32 devices in a mesh: grp: 2 (over y), evt: 4 (over z), var: 2 (over x), chan: 2 (over core).
Axes of the slice: x: 2, y: 2, z: 4, core: 2. Of those that a mesh axis runs over, the one named last changes fastest.
Arguments:
- variation_weights: bfloat16 [2, 32768, 1024], P('chan', ('grp', 'evt'), 'var'), parts along dimension 1, may hold values from -6 to 6
- bin_response: bfloat16 [2, 32768, 128], P('chan', ('grp', 'evt')), parts along dimension 1, may hold values from 0 to 0.25
- bin_block: int32 [2, 256], P('chan', ('grp', 'evt')), parts along dimension 1, may hold values from 0 to 127
- variation_coefficient: float32 [1024], replicated, may hold values from -4 to 4
- nuisance_index: int32 [1024], replicated, may hold values from 0 to 511, as said below
- expected: float32 [2, 32768], P('chan', ('grp', 'evt', 'var')), parts along dimension 1, may hold values from 1 to 16
- excess_counts: float32 [2, 32768], P('chan', ('grp', 'evt', 'var')), parts along dimension 1, may hold values from -10 to 10
Outputs:
- templates: float32 [2, 32768, 1024], P('chan', ('grp', 'evt', 'var')), parts along dimension 1
- nuisance_pulls: float32 [1024], P('grp'), parts along dimension 0
The draws below stay inside these ranges and needn't reach their ends.
There are 2 independent parts, one for each index of `grp`. The reference program is written for one: setup_inputs(seed, part) draws one part's arguments, and reference() takes and returns one part's arrays. A program takes and returns all parts, laid end to end along the dimension named above; an argument that names none is the same for every part. Nothing has to cross between parts.
Inputs may be any that keep to these rules, and one draw needn't show every extreme that they name: `nuisance_index`: each of the 512 nuisances is named by exactly 2 variations.
All inputs are finite; a program needn't handle non-finite values.
Results may differ from the reference program's by a relative error of at most 0.0085.
Values may be sent and summed in bfloat16 or wider, within the bound.
A program may use at most 128 MiB of HBM per device.

```python
import math
import jax
import jax.numpy as jnp
from jax import lax

BLK = 128
CH_BINS = 16384
VARS = 1024
NUIS = 512
EV_DEV = 4096
CHANNELS = 2
EV_CH = 16384
BLOCKS_CH = 128
N_EVT = 4


def draw_nuisance_index(key, part):
    order = jax.random.permutation(key, VARS)
    return (order % NUIS).astype(jnp.int32)


def place_ends(result, own_key, least, top_value):
    longest = result.shape.index(max(result.shape))
    spots = []
    for shift in (0, 1):
        where = [jax.random.randint(jax.random.fold_in(own_key, axis), (), 0, length) for axis, length in enumerate(result.shape)]
        where[longest] = (where[longest] + shift) % result.shape[longest]
        spots.append(tuple(where))
    return result.at[spots[0]].set(least).at[spots[1]].set(top_value)


def steps_of(rng, extent, split, smallest, high):
    loudness = 1.0
    for axis_at, blocks in split:
        heights = jax.random.uniform(jax.random.fold_in(jax.random.fold_in(rng, 6), axis_at), (blocks,), jnp.float32, smallest / len(split), high / len(split))
        loudness = loudness * jnp.repeat(jnp.exp(heights), extent[axis_at] // blocks).reshape((-1,) + (1,) * (len(extent) - 1 - axis_at))
    return loudness


def normal_values(own_key, extent, spread, limit, split=(), kind=jnp.bfloat16):
    result = jax.random.normal(own_key, extent, jnp.float32) * spread
    if len(split) > 0:
        result = steps_of(own_key, extent, split, -0.22, 0.18) * result
    return jnp.clip(result, min=-limit, max=limit).astype(kind)


def setup_inputs(seed: int = 0, part: int = 0) -> dict:
    key_list = jax.random.split(jax.random.key(seed), 8)
    part_splits = jax.random.split(jax.random.fold_in(key_list[7], part), 8)
    return {
        "variation_weights": normal_values(part_splits[0], (CHANNELS, EV_CH, VARS), 1.0, 6.0, ((0, 2), (1, 4), (2, 2))),
        "bin_response": jnp.clip(0.25 * jax.random.uniform(part_splits[1], (CHANNELS, EV_CH, BLK), jnp.float32) ** steps_of(part_splits[1], (CHANNELS, EV_CH, BLK), ((0, 2), (1, 4)), -0.2, 0.2), 0.0, 0.25).astype(jnp.bfloat16),
        "bin_block": place_ends(jax.random.randint(part_splits[2], (CHANNELS, BLOCKS_CH), 0, CH_BINS // BLK), jax.random.fold_in(part_splits[2], 1), 0, (CH_BINS // BLK) - 1).astype(jnp.int32),
        "variation_coefficient": normal_values(key_list[3], (VARS,), 1.0, 4.0, (), jnp.float32),
        "nuisance_index": draw_nuisance_index(jax.random.fold_in(key_list[7], 71), part),
        "expected": jnp.clip(jnp.exp(math.log(16.0) - 2.7725887 * jax.random.uniform(part_splits[5], (CHANNELS, CH_BINS), jnp.float32) ** steps_of(part_splits[5], (CHANNELS, CH_BINS), ((0, 2), (1, 8)), -0.2, 0.2)), 1.0, 16.0),
        "excess_counts": normal_values(part_splits[6], (CHANNELS, CH_BINS), 2.0, 10.0, ((0, 2), (1, 8)), jnp.float32),
    }


def shard_term(response, weights, blocks):
    nblocks = blocks.shape[0]
    resp_blocks = response.astype(jnp.float32).reshape(nblocks, BLK, BLK)
    weight_blocks = weights.astype(jnp.float32).reshape(nblocks, BLK, VARS)
    products = jnp.einsum('ket,kev->ktv', resp_blocks, weight_blocks, precision=lax.Precision.HIGHEST)
    summed = jax.ops.segment_sum(products, blocks.astype(jnp.int32), num_segments=CH_BINS // BLK)
    return summed.reshape(CH_BINS, VARS).astype(jnp.bfloat16)

def channel_templates(response, weights, blocks):
    resp_shards = response.reshape(N_EVT, EV_DEV, BLK)
    weight_shards = weights.reshape(N_EVT, EV_DEV, VARS)
    block_shards = blocks.reshape(N_EVT, EV_DEV // BLK)

    def add_shard(running, pieces):
        return (running + shard_term(pieces[0], pieces[1], pieces[2]).astype(jnp.float32), None)
    running, unused = lax.scan(add_shard, jnp.zeros((CH_BINS, VARS), jnp.float32), (resp_shards, weight_shards, block_shards))
    return running

def reference(variation_weights, bin_response, bin_block, variation_coefficient, nuisance_index, expected, excess_counts):
    templates = jnp.stack([channel_templates(bin_response[c], variation_weights[c], bin_block[c]) for c in range(CHANNELS)])
    mixing = (nuisance_index[:, None] == lax.iota(jnp.int32, NUIS)[None, :]).astype(jnp.float32) * variation_coefficient[:, None]
    flat_templates = templates.reshape(CHANNELS * CH_BINS, VARS)
    jacobian = jnp.dot(flat_templates, mixing, precision=lax.Precision.HIGHEST)
    inverse = 1.0 / expected.reshape(-1)
    scaled = jacobian * inverse[:, None]
    gram_matrix = lax.dot_general(scaled, jacobian, (((0,), (0,)), ((), ())), precision=lax.Precision.HIGHEST)
    gram_matrix = gram_matrix + jnp.eye(NUIS, dtype=jnp.float32)
    gradient = jnp.dot(excess_counts.reshape(-1) * inverse, jacobian, precision=lax.Precision.HIGHEST)
    factor = jnp.linalg.cholesky(gram_matrix)
    step_sizes = jax.scipy.linalg.cho_solve((factor, True), gradient)
    nuisance_pulls = step_sizes * jnp.sqrt(jnp.diagonal(gram_matrix))
    return (templates, nuisance_pulls)
```

```python
import functools

import jax
import jax.numpy as jnp
from jax import lax
from jax.experimental import pallas as pl
from jax.experimental.pallas import tpu as pltpu
from jax.sharding import PartitionSpec as P

BLK = 128
CH_BINS = 16384
NUIS = 512
BF = jnp.bfloat16
F32 = jnp.float32
HI = lax.Precision.HIGHEST


def transposed_dot(a, b):
    return lax.dot_general(a, b, (((0,), (0,)), ((), ())), preferred_element_type=F32)


def product_kernel(group, chunks, response_ref, weights_ref, *out_refs):
    for k in range(group):
        rows = slice(k * BLK, (k + 1) * BLK)
        prod = transposed_dot(response_ref[rows, :], weights_ref[rows, :]).astype(BF)
        for c in range(chunks):
            out_refs[c][k] = prod[:, c * BLK : (c + 1) * BLK]


def products_of(response, weights):
    events, var_local = weights.shape
    nblocks = events // BLK
    chunks = var_local // BLK
    group = 8
    return pl.pallas_call(
        functools.partial(product_kernel, group, chunks),
        grid=(nblocks // group,),
        in_specs=[
            pl.BlockSpec((group * BLK, BLK), lambda i: (i, 0)),
            pl.BlockSpec((group * BLK, var_local), lambda i: (i, 0)),
        ],
        out_specs=[pl.BlockSpec((group, BLK, BLK), lambda i: (i, 0, 0))] * chunks,
        out_shape=[jax.ShapeDtypeStruct((nblocks, BLK, BLK), BF)] * chunks,
        name="products",
    )(response, weights)


def dense_kernel(count, nblocks, with_extra, slots_ref, *refs):
    ins = refs[:count]
    rest = refs[count:]
    if with_extra:
        extra_ref, rest = rest[0], rest[1:]
    *outs, acc = rest
    if with_extra:
        acc[...] = extra_ref[...].astype(F32)
    else:
        acc[...] = jnp.zeros_like(acc)
    for s in range(count):

        def add(k, carry, s=s):
            slot = slots_ref[s * nblocks + k]

            @pl.when(slot >= 0)
            def _():
                acc[slot] = acc[slot] + ins[s][k].astype(F32)

            return carry

        lax.fori_loop(0, nblocks, add, 0)
    at = 0
    for out in outs:
        out[...] = acc[at : at + out.shape[0]].astype(BF)
        at += out.shape[0]


def dense_of(pieces, slots, out_blocks, extra=None):
    nblocks = pieces[0].shape[0]
    total = sum(out_blocks)
    operands = list(pieces) + ([] if extra is None else [extra])
    moved = sum(x.size for x in operands) * 2 + total * BLK * BLK * 2
    return pl.pallas_call(
        functools.partial(dense_kernel, len(pieces), nblocks, extra is not None),
        in_specs=[pl.BlockSpec(memory_space=pltpu.SMEM)]
        + [pl.BlockSpec(memory_space=pltpu.VMEM)] * len(operands),
        out_specs=[pl.BlockSpec(memory_space=pltpu.VMEM)] * len(out_blocks),
        out_shape=[jax.ShapeDtypeStruct((n, BLK, BLK), BF) for n in out_blocks],
        scratch_shapes=[pltpu.VMEM((total, BLK, BLK), F32)],
        compiler_params=pltpu.CompilerParams(vmem_limit_bytes=24 << 20),
        cost_estimate=pl.CostEstimate(flops=moved * 4, bytes_accessed=moved, transcendentals=0),
        name="dense",
    )(slots.reshape(-1), *operands)


def exchange_line(response, weights, blocks):
    z = lax.axis_index("evt")
    x = lax.axis_index("var")
    per_evt = CH_BINS // BLK // 4
    half = per_evt // 2
    pieces = products_of(response, weights)
    ids = lax.all_gather(blocks, "evt")
    nothing = jnp.full_like(blocks, -1)

    def held(ok, src):
        return jnp.where(ok, ids[src], nothing)

    sources = jnp.stack(
        [
            blocks,
            held((z == 1) | (z == 2), jnp.maximum(z - 1, 0)),
            held((z == 1) | (z == 2), jnp.minimum(z + 1, 3)),
            held(z == 2, 0),
            held(z == 1, 3),
        ]
    )
    rel = sources - z * per_evt
    inside = (sources >= 0) & (rel >= 0) & (rel < per_evt)
    final_slots = jnp.where(inside, (rel + x * half) % per_evt, -1)
    end = jnp.where(z == 1, 0, 3)
    rel_end = sources - end * per_evt
    from_left = jnp.array([1, 1, 0, 1, 0], jnp.int32)[:, None]
    from_right = jnp.array([1, 0, 1, 0, 1], jnp.int32)[:, None]
    use = jnp.where(z == 1, from_right, jnp.where(z == 2, from_left, 0))
    inside_end = (use > 0) & (sources >= 0) & (rel_end >= 0) & (rel_end < per_evt)
    end_slots = jnp.where(inside_end, (rel_end + x * half) % per_evt, -1)

    own, other = [], []
    previous = None
    for piece in pieces:
        if previous is not None:
            piece, _ = lax.optimization_barrier((piece, previous))
        right1 = lax.ppermute(piece, "evt", [(0, 1), (1, 2)])
        left1 = lax.ppermute(piece, "evt", [(3, 2), (2, 1)])
        right2 = lax.ppermute(right1, "evt", [(1, 2)])
        left2 = lax.ppermute(left1, "evt", [(2, 1)])
        previous = (right1, left1)
        buffers = [piece, right1, left1, right2, left2]
        (to_end,) = dense_of(buffers, end_slots, [per_evt])
        at_end = lax.ppermute(to_end, "evt", [(1, 0), (2, 3)])
        mine, theirs = dense_of(buffers, final_slots, [half, half], extra=at_end)
        own.append(mine)
        other.append(lax.ppermute(theirs, "var", [(0, 1), (1, 0)]))
    return own, other


def column_of(row):
    return jnp.broadcast_to(row, (BLK, row.shape[1])).T


def fit_kernel(chunks, tile, *refs):
    own, other = refs[:chunks], refs[chunks : 2 * chunks]
    place_ref, hi_ref, lo_ref, expected_ref, excess_ref, out_ref, gram_ref = refs[2 * chunks :]
    jac = jnp.zeros((tile, NUIS), F32)
    width = chunks * BLK
    for c in range(2 * chunks):
        if c < chunks:
            piece = own[c][...]
            at = place_ref[0] * width + c * BLK
        else:
            piece = other[c - chunks][...]
            at = (1 - place_ref[0]) * width + (c - chunks) * BLK
        at = pl.multiple_of(at, BLK)
        piece = piece.reshape(tile, BLK)
        out_ref[0, :, pl.ds(at, BLK)] = piece.astype(F32)
    temp = out_ref[0].astype(BF)
    jac = jnp.dot(temp, hi_ref[...], preferred_element_type=F32)
    jac = jac + jnp.dot(temp, lo_ref[...], preferred_element_type=F32)
    inverse = 1.0 / expected_ref[0]
    scale = jnp.concatenate([column_of(inverse)] * (NUIS // BLK), axis=1)
    pull = jnp.concatenate([column_of(inverse * excess_ref[0])] * (NUIS // BLK), axis=1)
    scaled = jac * scale
    jh = jac.astype(BF)
    jl = (jac - jh.astype(F32)).astype(BF)
    sh = scaled.astype(BF)
    sl = (scaled - sh.astype(F32)).astype(BF)
    gram = transposed_dot(sh, jh) + transposed_dot(sh, jl) + transposed_dot(sl, jh)
    grad = jnp.sum(jac * pull, axis=0, keepdims=True)

    @pl.when(pl.program_id(0) == 0)
    def _():
        gram_ref[...] = jnp.zeros_like(gram_ref)

    gram_ref[:NUIS, :] += gram
    gram_ref[NUIS:, :] += jnp.broadcast_to(grad, (8, NUIS))


def fit_of(own, other, place, hi, lo, expected, excess):
    chunks = len(own)
    bins = own[0].shape[0] * BLK
    tile = 512
    variations = 2 * chunks * BLK
    blocks = tile // BLK
    chunk_spec = pl.BlockSpec((blocks, BLK, BLK), lambda i: (i, 0, 0))
    row_spec = pl.BlockSpec((1, 1, tile), lambda i: (i, 0, 0))
    mix_spec = pl.BlockSpec((variations, NUIS), lambda i: (0, 0))
    return pl.pallas_call(
        functools.partial(fit_kernel, chunks, tile),
        grid=(bins // tile,),
        in_specs=[chunk_spec] * (2 * chunks)
        + [pl.BlockSpec(memory_space=pltpu.SMEM), mix_spec, mix_spec, row_spec, row_spec],
        out_specs=[
            pl.BlockSpec((1, tile, variations), lambda i: (0, i, 0)),
            pl.BlockSpec((NUIS + 8, NUIS), lambda i: (0, 0)),
        ],
        out_shape=[
            jax.ShapeDtypeStruct((1, bins, variations), F32),
            jax.ShapeDtypeStruct((NUIS + 8, NUIS), F32),
        ],
        compiler_params=pltpu.CompilerParams(vmem_limit_bytes=40 << 20),
        name="fit",
    )(
        *own,
        *other,
        place,
        hi,
        lo,
        expected.reshape(bins // tile, 1, tile),
        excess.reshape(bins // tile, 1, tile),
    )


def swept(a):
    rows = lax.broadcasted_iota(jnp.int32, (BLK, BLK), 0)
    lanes = lax.broadcasted_iota(jnp.int32, (BLK, BLK), 1)
    for k in range(BLK):
        row = a[k : k + 1, :]
        col = a[:, k : k + 1]
        inv = 1.0 / a[k : k + 1, k : k + 1]
        lane_k = lanes[:1] == k
        scaled_row = jnp.where(lane_k, -inv, row * inv)
        kept = jnp.where(lane_k, 0.0, a)
        a = jnp.where(rows == k, scaled_row, kept - col * jnp.where(lane_k, -inv, row * inv))
    return -a


def solve_kernel(gram_ref, out_ref, mat_ref):
    rows = lax.broadcasted_iota(jnp.int32, (NUIS, NUIS), 0)
    lanes = lax.broadcasted_iota(jnp.int32, (NUIS, NUIS), 1)
    on_diagonal = rows == lanes
    gram = gram_ref[:NUIS, :] + jnp.where(on_diagonal, 1.0, 0.0)
    diagonal = jnp.sum(jnp.where(on_diagonal, gram, 0.0), axis=0, keepdims=True)
    mat_ref[:, :NUIS] = gram
    mat_ref[:, NUIS:] = column_of(gram_ref[NUIS : NUIS + 1, :])

    def eliminate(j, carry):
        at = pl.multiple_of(j * BLK, BLK)
        inverse = swept(mat_ref[pl.ds(at, BLK), pl.ds(at, BLK)])
        pivot = jnp.dot(
            inverse, mat_ref[pl.ds(at, BLK), :], precision=HI, preferred_element_type=F32
        )
        factor = mat_ref[:, pl.ds(at, BLK)]
        block_of_row = lax.broadcasted_iota(jnp.int32, (NUIS, BLK), 0) // BLK
        factor = jnp.where(block_of_row == j, 0.0, factor)
        mat_ref[...] = mat_ref[...] - jnp.dot(
            factor, pivot, precision=HI, preferred_element_type=F32
        )
        mat_ref[pl.ds(at, BLK), :] = pivot
        return carry

    lax.fori_loop(0, NUIS // BLK, eliminate, 0)
    steps = mat_ref[:, NUIS:].T[:8]
    out_ref[...] = steps * jnp.sqrt(diagonal)


def pulls_of(gram):
    out = pl.pallas_call(
        solve_kernel,
        in_specs=[pl.BlockSpec(memory_space=pltpu.VMEM)],
        out_specs=pl.BlockSpec(memory_space=pltpu.VMEM),
        out_shape=jax.ShapeDtypeStruct((8, NUIS), F32),
        scratch_shapes=[pltpu.VMEM((NUIS, NUIS + BLK), F32)],
        compiler_params=pltpu.CompilerParams(vmem_limit_bytes=24 << 20),
        name="solve",
    )(gram)
    return out[0]


def exchange_any(response, weights, blocks):
    evt_count = lax.axis_size("evt")
    nblocks = blocks.shape[0]
    var_local = weights.shape[1]
    products = jnp.einsum(
        "ket,kev->ktv",
        response.reshape(nblocks, BLK, BLK),
        weights.reshape(nblocks, BLK, var_local),
        preferred_element_type=F32,
    )
    targets = lax.iota(jnp.int32, CH_BINS // evt_count * evt_count // BLK)
    select = (blocks[None, :] == targets[:, None]).astype(F32)
    block_term = jnp.einsum("qk,ktv->qtv", select, products, precision=HI)
    summed = lax.psum_scatter(
        block_term.reshape(CH_BINS, var_local).astype(BF), "evt", scatter_dimension=0, tiled=True
    )
    return lax.all_to_all(summed, "var", split_axis=0, concat_axis=1, tiled=True).astype(F32)


def fit_any(templates, mixing, expected, excess):
    jacobian = jnp.dot(templates, mixing, precision=HI)
    inverse = 1.0 / expected
    gram = lax.dot_general(
        jacobian * inverse[:, None], jacobian, (((0,), (0,)), ((), ())), precision=HI
    )
    gradient = jnp.dot(excess * inverse, jacobian, precision=HI)
    return jnp.concatenate([gram, jnp.broadcast_to(gradient[None], (8, NUIS))])


def shards(
    variation_weights,
    bin_response,
    bin_block,
    variation_coefficient,
    nuisance_index,
    expected,
    excess_counts,
):
    weights = variation_weights[0]
    response = bin_response[0]
    blocks = bin_block[0]
    mixing = (nuisance_index[:, None] == lax.iota(jnp.int32, NUIS)[None, :]).astype(
        F32
    ) * variation_coefficient[:, None]
    if lax.axis_size("evt") == 4 and lax.axis_size("var") == 2:
        own, other = exchange_line(response, weights, blocks)
        hi = mixing.astype(BF)
        lo = (mixing - hi.astype(F32)).astype(BF)
        place = lax.axis_index("var").astype(jnp.int32).reshape(1)
        templates, gram = fit_of(own, other, place, hi, lo, expected[0], excess_counts[0])
    else:
        templates = exchange_any(response, weights, blocks)
        gram = fit_any(templates, mixing, expected[0], excess_counts[0])
        templates = templates[None]
    gram = lax.psum(gram, ("evt", "var", "chan"))
    return (templates, pulls_of(gram))


def solution(mesh):
    placed = (
        P("chan", ("grp", "evt"), "var"),
        P("chan", ("grp", "evt"), None),
        P("chan", ("grp", "evt")),
        P(),
        P(),
        P("chan", ("grp", "evt", "var")),
        P("chan", ("grp", "evt", "var")),
    )
    return jax.shard_map(
        shards,
        mesh=mesh,
        in_specs=placed,
        out_specs=(P("chan", ("grp", "evt", "var"), None), P("grp")),
        check_vma=False,
    )
```

```python
import functools

import jax
import jax.numpy as jnp
from jax import lax
from jax.experimental import pallas as pl
from jax.experimental.pallas import tpu as pltpu
from jax.sharding import PartitionSpec as P

BLK = 128
CH_BINS = 16384
NUIS = 512
BF = jnp.bfloat16
F32 = jnp.float32
HI = lax.Precision.HIGHEST


def transposed_dot(a, b):
    return lax.dot_general(a, b, (((0,), (0,)), ((), ())), preferred_element_type=F32)


def product_kernel(group, chunks, response_ref, weights_ref, *out_refs):
    for k in range(group):
        rows = slice(k * BLK, (k + 1) * BLK)
        prod = transposed_dot(response_ref[rows, :], weights_ref[rows, :]).astype(BF)
        for c in range(chunks):
            out_refs[c][k] = prod[:, c * BLK : (c + 1) * BLK]


def products_of(response, weights):
    events, var_local = weights.shape
    nblocks = events // BLK
    chunks = var_local // BLK
    group = 8
    return pl.pallas_call(
        functools.partial(product_kernel, group, chunks),
        grid=(nblocks // group,),
        in_specs=[
            pl.BlockSpec((group * BLK, BLK), lambda i: (i, 0)),
            pl.BlockSpec((group * BLK, var_local), lambda i: (i, 0)),
        ],
        out_specs=[pl.BlockSpec((group, BLK, BLK), lambda i: (i, 0, 0))] * chunks,
        out_shape=[jax.ShapeDtypeStruct((nblocks, BLK, BLK), BF)] * chunks,
        name="products",
    )(response, weights)


def dense_kernel(count, nblocks, with_extra, slots_ref, *refs):
    ins = refs[:count]
    rest = refs[count:]
    if with_extra:
        extra_ref, rest = rest[0], rest[1:]
    *outs, acc = rest
    if with_extra:
        acc[...] = extra_ref[...].astype(F32)
    else:
        acc[...] = jnp.zeros_like(acc)
    for s in range(count):

        def add(k, carry, s=s):
            slot = slots_ref[s * nblocks + k]

            @pl.when(slot >= 0)
            def _():
                acc[slot] = acc[slot] + ins[s][k].astype(F32)

            return carry

        lax.fori_loop(0, nblocks, add, 0)
    at = 0
    for out in outs:
        out[...] = acc[at : at + out.shape[0]].astype(BF)
        at += out.shape[0]


def dense_of(pieces, slots, out_blocks, extra=None):
    nblocks = pieces[0].shape[0]
    total = sum(out_blocks)
    operands = list(pieces) + ([] if extra is None else [extra])
    moved = sum(x.size for x in operands) * 2 + total * BLK * BLK * 2
    return pl.pallas_call(
        functools.partial(dense_kernel, len(pieces), nblocks, extra is not None),
        in_specs=[pl.BlockSpec(memory_space=pltpu.SMEM)]
        + [pl.BlockSpec(memory_space=pltpu.VMEM)] * len(operands),
        out_specs=[pl.BlockSpec(memory_space=pltpu.VMEM)] * len(out_blocks),
        out_shape=[jax.ShapeDtypeStruct((n, BLK, BLK), BF) for n in out_blocks],
        scratch_shapes=[pltpu.VMEM((total, BLK, BLK), F32)],
        compiler_params=pltpu.CompilerParams(vmem_limit_bytes=24 << 20),
        cost_estimate=pl.CostEstimate(flops=moved * 4, bytes_accessed=moved, transcendentals=0),
        name="dense",
    )(slots.reshape(-1), *operands)


def exchange_line(response, weights, blocks):
    z = lax.axis_index("evt")
    x = lax.axis_index("var")
    per_evt = CH_BINS // BLK // 4
    half = per_evt // 2
    pieces = products_of(response, weights)
    nothing = jnp.full_like(blocks, -1)
    ids_right1 = lax.ppermute(blocks, "evt", [(0, 1), (1, 2)])
    ids_left1 = lax.ppermute(blocks, "evt", [(3, 2), (2, 1)])
    ids_right2 = lax.ppermute(ids_right1, "evt", [(1, 2)])
    ids_left2 = lax.ppermute(ids_left1, "evt", [(2, 1)])
    middle = (z == 1) | (z == 2)

    sources = jnp.stack(
        [
            blocks,
            jnp.where(middle, ids_right1, nothing),
            jnp.where(middle, ids_left1, nothing),
            jnp.where(z == 2, ids_right2, nothing),
            jnp.where(z == 1, ids_left2, nothing),
        ]
    )
    rel = sources - z * per_evt
    inside = (sources >= 0) & (rel >= 0) & (rel < per_evt)
    final_slots = jnp.where(inside, (rel + x * half) % per_evt, -1)
    end = jnp.where(z == 1, 0, 3)
    rel_end = sources - end * per_evt
    from_left = jnp.array([1, 1, 0, 1, 0], jnp.int32)[:, None]
    from_right = jnp.array([1, 0, 1, 0, 1], jnp.int32)[:, None]
    use = jnp.where(z == 1, from_right, jnp.where(z == 2, from_left, 0))
    inside_end = (use > 0) & (sources >= 0) & (rel_end >= 0) & (rel_end < per_evt)
    end_slots = jnp.where(inside_end, (rel_end + x * half) % per_evt, -1)

    own, other = [], []
    first_hops, second_hops, ends = [], [], []
    for c, piece in enumerate(pieces):
        ahead = first_hops[c - 1 : c] + second_hops[: max(c - 1, 0)][-1:] + ends[: max(c - 2, 0)][-1:]
        if ahead:
            piece, _ = lax.optimization_barrier((piece, ahead))
        right1 = lax.ppermute(piece, "evt", [(0, 1), (1, 2)])
        left1 = lax.ppermute(piece, "evt", [(3, 2), (2, 1)])
        right2 = lax.ppermute(right1, "evt", [(1, 2)])
        left2 = lax.ppermute(left1, "evt", [(2, 1)])
        first_hops.append((right1, left1))
        second_hops.append((right2, left2))
        buffers = [piece, right1, left1, right2, left2]
        (to_end,) = dense_of(buffers, end_slots, [per_evt])
        at_end = lax.ppermute(to_end, "evt", [(1, 0), (2, 3)])
        ends.append(at_end)
        mine, theirs = dense_of(buffers, final_slots, [half, half], extra=at_end)
        own.append(mine)
        other.append(lax.ppermute(theirs, "var", [(0, 1), (1, 0)]))
    return own, other


SIDE = NUIS // BLK
PACKED = 384


def packed_at(i, j):
    n = sum(SIDE - k for k in range(i)) + j - i
    return n // SIDE * BLK, n % SIDE * BLK


def grad_at(i):
    n = SIDE * (SIDE + 1) // 2
    return n // SIDE * BLK + 8 * i, n % SIDE * BLK


def column_of(row):
    return jnp.broadcast_to(row, (BLK, row.shape[1])).T


def fit_kernel(chunks, tile, *refs):
    own, other = refs[:chunks], refs[chunks : 2 * chunks]
    place_ref, hi_ref, lo_ref, expected_ref, excess_ref, out_ref, gram_ref = refs[2 * chunks :]
    jac = jnp.zeros((tile, NUIS), F32)
    width = chunks * BLK
    for c in range(2 * chunks):
        if c < chunks:
            piece = own[c][...]
            at = place_ref[0] * width + c * BLK
        else:
            piece = other[c - chunks][...]
            at = (1 - place_ref[0]) * width + (c - chunks) * BLK
        at = pl.multiple_of(at, BLK)
        piece = piece.reshape(tile, BLK)
        out_ref[0, :, pl.ds(at, BLK)] = piece.astype(F32)
    temp = out_ref[0].astype(BF)
    jac = jnp.dot(temp, hi_ref[...], preferred_element_type=F32)
    jac = jac + jnp.dot(temp, lo_ref[...], preferred_element_type=F32)
    inverse = 1.0 / expected_ref[0]
    scale = jnp.concatenate([column_of(inverse)] * (NUIS // BLK), axis=1)
    pull = jnp.concatenate([column_of(inverse * excess_ref[0])] * (NUIS // BLK), axis=1)
    scaled = jac * scale
    jh = jac.astype(BF)
    jl = (jac - jh.astype(F32)).astype(BF)
    sh = scaled.astype(BF)
    sl = (scaled - sh.astype(F32)).astype(BF)
    grad = jnp.sum(jac * pull, axis=0, keepdims=True)

    @pl.when(pl.program_id(0) == 0)
    def _():
        gram_ref[...] = jnp.zeros_like(gram_ref)

    for i in range(SIDE):
        left = slice(i * BLK, (i + 1) * BLK)
        right = slice(i * BLK, NUIS)
        part = transposed_dot(sh[:, left], jh[:, right])
        part = part + transposed_dot(sh[:, left], jl[:, right])
        part = part + transposed_dot(sl[:, left], jh[:, right])
        for j in range(i, SIDE):
            row, lane = packed_at(i, j)
            gram_ref[row : row + BLK, lane : lane + BLK] += part[:, (j - i) * BLK : (j - i + 1) * BLK]
        row, lane = grad_at(i)
        gram_ref[row : row + 8, lane : lane + BLK] += jnp.broadcast_to(grad[:, left], (8, BLK))


def fit_of(own, other, place, hi, lo, expected, excess):
    chunks = len(own)
    bins = own[0].shape[0] * BLK
    tile = 512
    variations = 2 * chunks * BLK
    blocks = tile // BLK
    chunk_spec = pl.BlockSpec((blocks, BLK, BLK), lambda i: (i, 0, 0))
    row_spec = pl.BlockSpec((1, 1, tile), lambda i: (i, 0, 0))
    mix_spec = pl.BlockSpec((variations, NUIS), lambda i: (0, 0))
    return pl.pallas_call(
        functools.partial(fit_kernel, chunks, tile),
        grid=(bins // tile,),
        in_specs=[chunk_spec] * (2 * chunks)
        + [pl.BlockSpec(memory_space=pltpu.SMEM), mix_spec, mix_spec, row_spec, row_spec],
        out_specs=[
            pl.BlockSpec((1, tile, variations), lambda i: (0, i, 0)),
            pl.BlockSpec((PACKED, NUIS), lambda i: (0, 0)),
        ],
        out_shape=[
            jax.ShapeDtypeStruct((1, bins, variations), F32),
            jax.ShapeDtypeStruct((PACKED, NUIS), F32),
        ],
        compiler_params=pltpu.CompilerParams(vmem_limit_bytes=40 << 20),
        name="fit",
    )(
        *own,
        *other,
        place,
        hi,
        lo,
        expected.reshape(bins // tile, 1, tile),
        excess.reshape(bins // tile, 1, tile),
    )


def swept(a):
    rows = lax.broadcasted_iota(jnp.int32, (BLK, BLK), 0)
    lanes = lax.broadcasted_iota(jnp.int32, (BLK, BLK), 1)
    for k in range(BLK):
        row = a[k : k + 1, :]
        col = a[:, k : k + 1]
        inv = 1.0 / a[k : k + 1, k : k + 1]
        lane_k = lanes[:1] == k
        scaled_row = jnp.where(lane_k, -inv, row * inv)
        kept = jnp.where(lane_k, 0.0, a)
        a = jnp.where(rows == k, scaled_row, kept - col * jnp.where(lane_k, -inv, row * inv))
    return -a


def solve_packed(packed_ref, out_ref, mat_ref):
    rows = lax.broadcasted_iota(jnp.int32, (BLK, BLK), 0)
    lanes = lax.broadcasted_iota(jnp.int32, (BLK, BLK), 1)
    on_diagonal = rows == lanes
    diagonal = []
    for i in range(SIDE):
        at = slice(i * BLK, (i + 1) * BLK)
        for j in range(i, SIDE):
            row, lane = packed_at(i, j)
            block = packed_ref[row : row + BLK, lane : lane + BLK]
            if i == j:
                block = block + jnp.where(on_diagonal, 1.0, 0.0)
                diagonal.append(
                    jnp.sum(jnp.where(on_diagonal, block, 0.0), axis=0, keepdims=True)
                )
                mat_ref[at, at] = block
            else:
                to = slice(j * BLK, (j + 1) * BLK)
                mat_ref[at, to] = block
                mat_ref[to, at] = block.T
        row, lane = grad_at(i)
        mat_ref[at, NUIS:] = column_of(packed_ref[row : row + 1, lane : lane + BLK])
    diagonal = jnp.concatenate(diagonal, axis=1)

    def eliminate(j, carry):
        at = pl.multiple_of(j * BLK, BLK)
        inverse = swept(mat_ref[pl.ds(at, BLK), pl.ds(at, BLK)])
        pivot = jnp.dot(
            inverse, mat_ref[pl.ds(at, BLK), :], precision=HI, preferred_element_type=F32
        )
        factor = mat_ref[:, pl.ds(at, BLK)]
        block_of_row = lax.broadcasted_iota(jnp.int32, (NUIS, BLK), 0) // BLK
        factor = jnp.where(block_of_row == j, 0.0, factor)
        mat_ref[...] = mat_ref[...] - jnp.dot(
            factor, pivot, precision=HI, preferred_element_type=F32
        )
        mat_ref[pl.ds(at, BLK), :] = pivot
        return carry

    lax.fori_loop(0, NUIS // BLK, eliminate, 0)
    steps = mat_ref[:, NUIS:].T[:8]
    out_ref[...] = steps * jnp.sqrt(diagonal)


def summed_solve_kernel(
    gram_ref, out_ref, buf, from_chan, from_var, from_evt, res, mat_ref, send_sem, recv_sem
):
    c, x, z = lax.axis_index("chan"), lax.axis_index("var"), lax.axis_index("evt")
    half, quarter, part = PACKED // 2, PACKED // 4, PACKED // 16
    over_chan, over_var = {"chan": 1 - c}, {"var": 1 - x}
    over_evt = [{"evt": lax.rem(z + d, 4)} for d in (1, 2, 3)]
    mesh_ids = pl.DeviceIdType.MESH

    barrier = pltpu.get_barrier_semaphore()
    for other in [over_chan, over_var] + over_evt:
        pl.semaphore_signal(barrier, inc=1, device_id=other, device_id_type=mesh_ids)
    pl.semaphore_wait(barrier, 5)

    def copy(n, src, dst, other):
        return pltpu.make_async_remote_copy(
            src_ref=src,
            dst_ref=dst,
            send_sem=send_sem.at[n],
            recv_sem=recv_sem.at[n],
            device_id=other,
            device_id_type=mesh_ids,
        )

    def rows(start, count):
        return pl.ds(pl.multiple_of(start, 8), count)

    half_at = c * half
    step = copy(0, gram_ref.at[rows((1 - c) * half, half)], from_chan, over_chan)
    step.start()
    step.wait()
    buf[...] = gram_ref[rows(half_at, half), :] + from_chan[...]
    step = copy(1, buf.at[rows((1 - x) * quarter, quarter)], from_var, over_var)
    step.start()
    step.wait()
    mine = buf.at[rows(x * quarter, quarter)]
    mine[...] = mine[...] + from_var[...]
    steps = []
    for d, other in enumerate(over_evt):
        target = lax.rem(z + d + 1, 4)
        at = rows(x * quarter + target * part, part)
        steps.append(copy(2 + d, buf.at[at], from_evt.at[d], other))
    for step in steps:
        step.start()
    for step in steps:
        step.wait()
    own_at = rows(half_at + x * quarter + z * part, part)
    total = buf[rows(x * quarter + z * part, part), :] + from_evt[0]
    res[own_at, :] = total + from_evt[1] + from_evt[2]
    steps = [copy(5 + d, res.at[own_at], res.at[own_at], o) for d, o in enumerate(over_evt)]
    for step in steps:
        step.start()
    for step in steps:
        step.wait()
    quarter_at = rows(half_at + x * quarter, quarter)
    step = copy(8, res.at[quarter_at], res.at[quarter_at], over_var)
    step.start()
    step.wait()
    half_rows = rows(half_at, half)
    step = copy(9, res.at[half_rows], res.at[half_rows], over_chan)
    step.start()
    step.wait()
    solve_packed(res, out_ref, mat_ref)


def pulls_summed(gram):
    half, quarter, part = PACKED // 2, PACKED // 4, PACKED // 16
    return pl.pallas_call(
        summed_solve_kernel,
        in_specs=[pl.BlockSpec(memory_space=pltpu.VMEM)],
        out_specs=pl.BlockSpec(memory_space=pltpu.VMEM),
        out_shape=jax.ShapeDtypeStruct((8, NUIS), F32),
        scratch_shapes=[
            pltpu.VMEM((half, NUIS), F32),
            pltpu.VMEM((half, NUIS), F32),
            pltpu.VMEM((quarter, NUIS), F32),
            pltpu.VMEM((3, part, NUIS), F32),
            pltpu.VMEM((PACKED, NUIS), F32),
            pltpu.VMEM((NUIS, NUIS + BLK), F32),
            pltpu.SemaphoreType.DMA((10,)),
            pltpu.SemaphoreType.DMA((10,)),
        ],
        compiler_params=pltpu.CompilerParams(
            collective_id=0, has_side_effects=True, vmem_limit_bytes=24 << 20
        ),
        name="sum_solve",
    )(gram)[0]


def pulls_of(gram):
    out = pl.pallas_call(
        solve_packed,
        in_specs=[pl.BlockSpec(memory_space=pltpu.VMEM)],
        out_specs=pl.BlockSpec(memory_space=pltpu.VMEM),
        out_shape=jax.ShapeDtypeStruct((8, NUIS), F32),
        scratch_shapes=[pltpu.VMEM((NUIS, NUIS + BLK), F32)],
        compiler_params=pltpu.CompilerParams(vmem_limit_bytes=24 << 20),
        name="solve",
    )(gram)
    return out[0]


def exchange_any(response, weights, blocks):
    evt_count = lax.axis_size("evt")
    nblocks = blocks.shape[0]
    var_local = weights.shape[1]
    products = jnp.einsum(
        "ket,kev->ktv",
        response.reshape(nblocks, BLK, BLK),
        weights.reshape(nblocks, BLK, var_local),
        preferred_element_type=F32,
    )
    targets = lax.iota(jnp.int32, CH_BINS // evt_count * evt_count // BLK)
    select = (blocks[None, :] == targets[:, None]).astype(F32)
    block_term = jnp.einsum("qk,ktv->qtv", select, products, precision=HI)
    summed = lax.psum_scatter(
        block_term.reshape(CH_BINS, var_local).astype(BF), "evt", scatter_dimension=0, tiled=True
    )
    return lax.all_to_all(summed, "var", split_axis=0, concat_axis=1, tiled=True).astype(F32)


def fit_any(templates, mixing, expected, excess):
    jacobian = jnp.dot(templates, mixing, precision=HI)
    inverse = 1.0 / expected
    gram = lax.dot_general(
        jacobian * inverse[:, None], jacobian, (((0,), (0,)), ((), ())), precision=HI
    )
    gradient = jnp.dot(excess * inverse, jacobian, precision=HI)
    packed = jnp.zeros((PACKED, NUIS), F32)
    for i in range(SIDE):
        for j in range(i, SIDE):
            row, lane = packed_at(i, j)
            block = gram[i * BLK : (i + 1) * BLK, j * BLK : (j + 1) * BLK]
            packed = packed.at[row : row + BLK, lane : lane + BLK].set(block)
        row, lane = grad_at(i)
        packed = packed.at[row : row + 8, lane : lane + BLK].set(
            gradient[None, i * BLK : (i + 1) * BLK]
        )
    return packed


def shards(
    variation_weights,
    bin_response,
    bin_block,
    variation_coefficient,
    nuisance_index,
    expected,
    excess_counts,
):
    weights = variation_weights[0]
    response = bin_response[0]
    blocks = bin_block[0]
    mixing = (nuisance_index[:, None] == lax.iota(jnp.int32, NUIS)[None, :]).astype(
        F32
    ) * variation_coefficient[:, None]
    if lax.axis_size("evt") == 4 and lax.axis_size("var") == 2:
        own, other = exchange_line(response, weights, blocks)
        hi = mixing.astype(BF)
        lo = (mixing - hi.astype(F32)).astype(BF)
        place = lax.axis_index("var").astype(jnp.int32).reshape(1)
        templates, gram = fit_of(own, other, place, hi, lo, expected[0], excess_counts[0])
        return (templates, pulls_summed(gram))
    else:
        templates = exchange_any(response, weights, blocks)
        gram = fit_any(templates, mixing, expected[0], excess_counts[0])
        templates = templates[None]
    gram = lax.psum(gram, ("evt", "var", "chan"))
    return (templates, pulls_of(gram))


def solution(mesh):
    placed = (
        P("chan", ("grp", "evt"), "var"),
        P("chan", ("grp", "evt"), None),
        P("chan", ("grp", "evt")),
        P(),
        P(),
        P("chan", ("grp", "evt", "var")),
        P("chan", ("grp", "evt", "var")),
    )
    return jax.shard_map(
        shards,
        mesh=mesh,
        in_specs=placed,
        out_specs=(P("chan", ("grp", "evt", "var"), None), P("grp")),
        check_vma=False,
    )
```

```python
import functools

import jax
import jax.numpy as jnp
from jax import lax
from jax.experimental import pallas as pl
from jax.experimental.pallas import tpu as pltpu
from jax.sharding import PartitionSpec as P

BLK = 128
CH_BINS = 16384
NUIS = 512
BF = jnp.bfloat16
F32 = jnp.float32
HI = lax.Precision.HIGHEST


def transposed_dot(a, b):
    return lax.dot_general(a, b, (((0,), (0,)), ((), ())), preferred_element_type=F32)


def product_kernel(group, chunks, response_ref, weights_ref, *out_refs):
    for k in range(group):
        rows = slice(k * BLK, (k + 1) * BLK)
        prod = transposed_dot(response_ref[rows, :], weights_ref[rows, :]).astype(BF)
        for c in range(chunks):
            out_refs[c][k] = prod[:, c * BLK : (c + 1) * BLK]


def products_of(response, weights):
    events, var_local = weights.shape
    nblocks = events // BLK
    chunks = var_local // BLK
    group = 8
    return pl.pallas_call(
        functools.partial(product_kernel, group, chunks),
        grid=(nblocks // group,),
        in_specs=[
            pl.BlockSpec((group * BLK, BLK), lambda i: (i, 0)),
            pl.BlockSpec((group * BLK, var_local), lambda i: (i, 0)),
        ],
        out_specs=[pl.BlockSpec((group, BLK, BLK), lambda i: (i, 0, 0))] * chunks,
        out_shape=[jax.ShapeDtypeStruct((nblocks, BLK, BLK), BF)] * chunks,
        name="products",
    )(response, weights)


def dense_kernel(count, nblocks, with_extra, slots_ref, *refs):
    ins = refs[:count]
    rest = refs[count:]
    if with_extra:
        extra_ref, rest = rest[0], rest[1:]
    *outs, acc = rest
    if with_extra:
        acc[...] = extra_ref[...].astype(F32)
    else:
        acc[...] = jnp.zeros_like(acc)
    for s in range(count):

        def add(k, carry, s=s):
            slot = slots_ref[s * nblocks + k]

            @pl.when(slot >= 0)
            def _():
                acc[slot] = acc[slot] + ins[s][k].astype(F32)

            return carry

        lax.fori_loop(0, nblocks, add, 0)
    at = 0
    for out in outs:
        out[...] = acc[at : at + out.shape[0]].astype(BF)
        at += out.shape[0]


def dense_of(pieces, slots, out_blocks, extra=None):
    nblocks = pieces[0].shape[0]
    total = sum(out_blocks)
    operands = list(pieces) + ([] if extra is None else [extra])
    moved = sum(x.size for x in operands) * 2 + total * BLK * BLK * 2
    return pl.pallas_call(
        functools.partial(dense_kernel, len(pieces), nblocks, extra is not None),
        in_specs=[pl.BlockSpec(memory_space=pltpu.SMEM)]
        + [pl.BlockSpec(memory_space=pltpu.VMEM)] * len(operands),
        out_specs=[pl.BlockSpec(memory_space=pltpu.VMEM)] * len(out_blocks),
        out_shape=[jax.ShapeDtypeStruct((n, BLK, BLK), BF) for n in out_blocks],
        scratch_shapes=[pltpu.VMEM((total, BLK, BLK), F32)],
        compiler_params=pltpu.CompilerParams(vmem_limit_bytes=24 << 20),
        cost_estimate=pl.CostEstimate(flops=moved * 4, bytes_accessed=moved, transcendentals=0),
        name="dense",
    )(slots.reshape(-1), *operands)


def exchange_line(response, weights, blocks):
    z = lax.axis_index("evt")
    x = lax.axis_index("var")
    per_evt = CH_BINS // BLK // 4
    half = per_evt // 2
    pieces = products_of(response, weights)
    nothing = jnp.full_like(blocks, -1)
    ids_right1 = lax.ppermute(blocks, "evt", [(0, 1), (1, 2)])
    ids_left1 = lax.ppermute(blocks, "evt", [(3, 2), (2, 1)])
    ids_right2 = lax.ppermute(ids_right1, "evt", [(1, 2)])
    ids_left2 = lax.ppermute(ids_left1, "evt", [(2, 1)])
    middle = (z == 1) | (z == 2)

    sources = jnp.stack(
        [
            blocks,
            jnp.where(middle, ids_right1, nothing),
            jnp.where(middle, ids_left1, nothing),
            jnp.where(z == 2, ids_right2, nothing),
            jnp.where(z == 1, ids_left2, nothing),
        ]
    )
    rel = sources - z * per_evt
    inside = (sources >= 0) & (rel >= 0) & (rel < per_evt)
    final_slots = jnp.where(inside, (rel + x * half) % per_evt, -1)
    end = jnp.where(z == 1, 0, 3)
    rel_end = sources - end * per_evt
    from_left = jnp.array([1, 1, 0, 1, 0], jnp.int32)[:, None]
    from_right = jnp.array([1, 0, 1, 0, 1], jnp.int32)[:, None]
    use = jnp.where(z == 1, from_right, jnp.where(z == 2, from_left, 0))
    inside_end = (use > 0) & (sources >= 0) & (rel_end >= 0) & (rel_end < per_evt)
    end_slots = jnp.where(inside_end, (rel_end + x * half) % per_evt, -1)

    own, other = [], []
    first_hops, ends, arrived = [], [], []
    for c, piece in enumerate(pieces):
        if c >= 2:
            piece, _ = lax.optimization_barrier((piece, first_hops[c - 2]))
        right1 = lax.ppermute(piece, "evt", [(0, 1), (1, 2)])
        left1 = lax.ppermute(piece, "evt", [(3, 2), (2, 1)])
        if c >= 2:
            right1, left1, _, _ = lax.optimization_barrier(
                (right1, left1, ends[c - 2], arrived[: c - 2])
            )
        right2 = lax.ppermute(right1, "evt", [(1, 2)])
        left2 = lax.ppermute(left1, "evt", [(2, 1)])
        first_hops.append((right1, left1))
        buffers = [piece, right1, left1, right2, left2]
        (to_end,) = dense_of(buffers, end_slots, [per_evt])
        ends.append(to_end)
        at_end = lax.ppermute(to_end, "evt", [(1, 0), (2, 3)])
        arrived.append(at_end)
        mine, theirs = dense_of(buffers, final_slots, [half, half], extra=at_end)
        own.append(mine)
        other.append(lax.ppermute(theirs, "var", [(0, 1), (1, 0)]))
    return own, other


SIDE = NUIS // BLK
PACKED = 384


def packed_at(i, j):
    n = sum(SIDE - k for k in range(i)) + j - i
    return n // SIDE * BLK, n % SIDE * BLK


def grad_at(i):
    n = SIDE * (SIDE + 1) // 2
    return n // SIDE * BLK + 8 * i, n % SIDE * BLK


def column_of(row):
    return jnp.broadcast_to(row, (BLK, row.shape[1])).T


def fit_kernel(chunks, tile, *refs):
    own, other = refs[:chunks], refs[chunks : 2 * chunks]
    place_ref, hi_ref, lo_ref, expected_ref, excess_ref, out_ref, gram_ref = refs[2 * chunks :]
    jac = jnp.zeros((tile, NUIS), F32)
    width = chunks * BLK
    for c in range(2 * chunks):
        if c < chunks:
            piece = own[c][...]
            at = place_ref[0] * width + c * BLK
        else:
            piece = other[c - chunks][...]
            at = (1 - place_ref[0]) * width + (c - chunks) * BLK
        at = pl.multiple_of(at, BLK)
        piece = piece.reshape(tile, BLK)
        out_ref[0, :, pl.ds(at, BLK)] = piece.astype(F32)
    temp = out_ref[0].astype(BF)
    jac = jnp.dot(temp, hi_ref[...], preferred_element_type=F32)
    jac = jac + jnp.dot(temp, lo_ref[...], preferred_element_type=F32)
    inverse = 1.0 / expected_ref[0]
    scale = jnp.concatenate([column_of(inverse)] * (NUIS // BLK), axis=1)
    pull = jnp.concatenate([column_of(inverse * excess_ref[0])] * (NUIS // BLK), axis=1)
    scaled = jac * scale
    jh = jac.astype(BF)
    jl = (jac - jh.astype(F32)).astype(BF)
    sh = scaled.astype(BF)
    sl = (scaled - sh.astype(F32)).astype(BF)
    grad = jnp.sum(jac * pull, axis=0, keepdims=True)

    @pl.when(pl.program_id(0) == 0)
    def _():
        gram_ref[...] = jnp.zeros_like(gram_ref)

    for i in range(SIDE):
        left = slice(i * BLK, (i + 1) * BLK)
        right = slice(i * BLK, NUIS)
        part = transposed_dot(sh[:, left], jh[:, right])
        part = part + transposed_dot(sh[:, left], jl[:, right])
        part = part + transposed_dot(sl[:, left], jh[:, right])
        for j in range(i, SIDE):
            row, lane = packed_at(i, j)
            gram_ref[row : row + BLK, lane : lane + BLK] += part[:, (j - i) * BLK : (j - i + 1) * BLK]
        row, lane = grad_at(i)
        gram_ref[row : row + 8, lane : lane + BLK] += jnp.broadcast_to(grad[:, left], (8, BLK))


def fit_of(own, other, place, hi, lo, expected, excess):
    chunks = len(own)
    bins = own[0].shape[0] * BLK
    tile = 512
    variations = 2 * chunks * BLK
    blocks = tile // BLK
    chunk_spec = pl.BlockSpec((blocks, BLK, BLK), lambda i: (i, 0, 0))
    row_spec = pl.BlockSpec((1, 1, tile), lambda i: (i, 0, 0))
    mix_spec = pl.BlockSpec((variations, NUIS), lambda i: (0, 0))
    return pl.pallas_call(
        functools.partial(fit_kernel, chunks, tile),
        grid=(bins // tile,),
        in_specs=[chunk_spec] * (2 * chunks)
        + [pl.BlockSpec(memory_space=pltpu.SMEM), mix_spec, mix_spec, row_spec, row_spec],
        out_specs=[
            pl.BlockSpec((1, tile, variations), lambda i: (0, i, 0)),
            pl.BlockSpec((PACKED, NUIS), lambda i: (0, 0)),
        ],
        out_shape=[
            jax.ShapeDtypeStruct((1, bins, variations), F32),
            jax.ShapeDtypeStruct((PACKED, NUIS), F32),
        ],
        compiler_params=pltpu.CompilerParams(vmem_limit_bytes=40 << 20),
        name="fit",
    )(
        *own,
        *other,
        place,
        hi,
        lo,
        expected.reshape(bins // tile, 1, tile),
        excess.reshape(bins // tile, 1, tile),
    )


def swept(a):
    rows = lax.broadcasted_iota(jnp.int32, (BLK, BLK), 0)
    lanes = lax.broadcasted_iota(jnp.int32, (BLK, BLK), 1)
    for k in range(0, BLK, 2):
        row1, row2 = a[k : k + 1, :], a[k + 1 : k + 2, :]
        col1, col2 = a[:, k : k + 1], a[:, k + 1 : k + 2]
        p, q = a[k : k + 1, k : k + 1], a[k : k + 1, k + 1 : k + 2]
        s = a[k + 1 : k + 2, k + 1 : k + 2]
        inv = 1.0 / p
        ratio = q * inv
        m22 = 1.0 / (s - q * ratio)
        m12 = -ratio * m22
        m11 = inv - ratio * m12
        at1, at2 = lanes[:1] == k, lanes[:1] == k + 1
        new1 = jnp.where(at1, -m11, jnp.where(at2, -m12, m11 * row1 + m12 * row2))
        new2 = jnp.where(at1, -m12, jnp.where(at2, -m22, m12 * row1 + m22 * row2))
        kept = jnp.where(at1 | at2, 0.0, a)
        a = kept - col1 * new1 - col2 * new2
        a = jnp.where(rows == k, new1, jnp.where(rows == k + 1, new2, a))
    return -a


def solve_packed(packed_ref, out_ref, mat_ref):
    rows = lax.broadcasted_iota(jnp.int32, (BLK, BLK), 0)
    lanes = lax.broadcasted_iota(jnp.int32, (BLK, BLK), 1)
    on_diagonal = rows == lanes
    diagonal = []
    for i in range(SIDE):
        at = slice(i * BLK, (i + 1) * BLK)
        for j in range(i, SIDE):
            row, lane = packed_at(i, j)
            block = packed_ref[row : row + BLK, lane : lane + BLK]
            if i == j:
                block = block + jnp.where(on_diagonal, 1.0, 0.0)
                diagonal.append(
                    jnp.sum(jnp.where(on_diagonal, block, 0.0), axis=0, keepdims=True)
                )
                mat_ref[at, at] = block
            else:
                to = slice(j * BLK, (j + 1) * BLK)
                mat_ref[at, to] = block
                mat_ref[to, at] = block.T
        row, lane = grad_at(i)
        mat_ref[at, NUIS:] = column_of(packed_ref[row : row + 1, lane : lane + BLK])
    diagonal = jnp.concatenate(diagonal, axis=1)

    def eliminate(j, carry):
        at = pl.multiple_of(j * BLK, BLK)
        inverse = swept(mat_ref[pl.ds(at, BLK), pl.ds(at, BLK)])
        pivot = jnp.dot(
            inverse, mat_ref[pl.ds(at, BLK), :], precision=HI, preferred_element_type=F32
        )
        factor = mat_ref[:, pl.ds(at, BLK)]
        block_of_row = lax.broadcasted_iota(jnp.int32, (NUIS, BLK), 0) // BLK
        factor = jnp.where(block_of_row == j, 0.0, factor)
        mat_ref[...] = mat_ref[...] - jnp.dot(
            factor, pivot, precision=HI, preferred_element_type=F32
        )
        mat_ref[pl.ds(at, BLK), :] = pivot
        return carry

    lax.fori_loop(0, NUIS // BLK, eliminate, 0)
    steps = mat_ref[:, NUIS:].T[:8]
    out_ref[...] = steps * jnp.sqrt(diagonal)


def summed_solve_kernel(
    gram_ref, out_ref, buf, from_chan, from_var, from_evt, res, mat_ref, send_sem, recv_sem
):
    c, x, z = lax.axis_index("chan"), lax.axis_index("var"), lax.axis_index("evt")
    half, quarter, part = PACKED // 2, PACKED // 4, PACKED // 16
    over_chan, over_var = {"chan": 1 - c}, {"var": 1 - x}
    over_evt = [{"evt": lax.rem(z + d, 4)} for d in (1, 2, 3)]
    mesh_ids = pl.DeviceIdType.MESH

    barrier = pltpu.get_barrier_semaphore()
    for other in [over_chan, over_var] + over_evt:
        pl.semaphore_signal(barrier, inc=1, device_id=other, device_id_type=mesh_ids)
    pl.semaphore_wait(barrier, 5)

    def copy(n, src, dst, other):
        return pltpu.make_async_remote_copy(
            src_ref=src,
            dst_ref=dst,
            send_sem=send_sem.at[n],
            recv_sem=recv_sem.at[n],
            device_id=other,
            device_id_type=mesh_ids,
        )

    def rows(start, count):
        return pl.ds(pl.multiple_of(start, 8), count)

    half_at = c * half
    step = copy(0, gram_ref.at[rows((1 - c) * half, half)], from_chan, over_chan)
    step.start()
    step.wait()
    buf[...] = gram_ref[rows(half_at, half), :] + from_chan[...]
    step = copy(1, buf.at[rows((1 - x) * quarter, quarter)], from_var, over_var)
    step.start()
    step.wait()
    mine = buf.at[rows(x * quarter, quarter)]
    mine[...] = mine[...] + from_var[...]
    steps = []
    for d, other in enumerate(over_evt):
        target = lax.rem(z + d + 1, 4)
        at = rows(x * quarter + target * part, part)
        steps.append(copy(2 + d, buf.at[at], from_evt.at[d], other))
    for step in steps:
        step.start()
    for step in steps:
        step.wait()
    own_at = rows(half_at + x * quarter + z * part, part)
    total = buf[rows(x * quarter + z * part, part), :] + from_evt[0]
    res[own_at, :] = total + from_evt[1] + from_evt[2]
    steps = [copy(5 + d, res.at[own_at], res.at[own_at], o) for d, o in enumerate(over_evt)]
    for step in steps:
        step.start()
    for step in steps:
        step.wait()
    quarter_at = rows(half_at + x * quarter, quarter)
    step = copy(8, res.at[quarter_at], res.at[quarter_at], over_var)
    step.start()
    step.wait()
    half_rows = rows(half_at, half)
    step = copy(9, res.at[half_rows], res.at[half_rows], over_chan)
    step.start()
    step.wait()
    solve_packed(res, out_ref, mat_ref)


def pulls_summed(gram):
    half, quarter, part = PACKED // 2, PACKED // 4, PACKED // 16
    return pl.pallas_call(
        summed_solve_kernel,
        in_specs=[pl.BlockSpec(memory_space=pltpu.VMEM)],
        out_specs=pl.BlockSpec(memory_space=pltpu.VMEM),
        out_shape=jax.ShapeDtypeStruct((8, NUIS), F32),
        scratch_shapes=[
            pltpu.VMEM((half, NUIS), F32),
            pltpu.VMEM((half, NUIS), F32),
            pltpu.VMEM((quarter, NUIS), F32),
            pltpu.VMEM((3, part, NUIS), F32),
            pltpu.VMEM((PACKED, NUIS), F32),
            pltpu.VMEM((NUIS, NUIS + BLK), F32),
            pltpu.SemaphoreType.DMA((10,)),
            pltpu.SemaphoreType.DMA((10,)),
        ],
        compiler_params=pltpu.CompilerParams(
            collective_id=0, has_side_effects=True, vmem_limit_bytes=24 << 20
        ),
        name="sum_solve",
    )(gram)[0]


def pulls_of(gram):
    out = pl.pallas_call(
        solve_packed,
        in_specs=[pl.BlockSpec(memory_space=pltpu.VMEM)],
        out_specs=pl.BlockSpec(memory_space=pltpu.VMEM),
        out_shape=jax.ShapeDtypeStruct((8, NUIS), F32),
        scratch_shapes=[pltpu.VMEM((NUIS, NUIS + BLK), F32)],
        compiler_params=pltpu.CompilerParams(vmem_limit_bytes=24 << 20),
        name="solve",
    )(gram)
    return out[0]


def exchange_any(response, weights, blocks):
    evt_count = lax.axis_size("evt")
    nblocks = blocks.shape[0]
    var_local = weights.shape[1]
    products = jnp.einsum(
        "ket,kev->ktv",
        response.reshape(nblocks, BLK, BLK),
        weights.reshape(nblocks, BLK, var_local),
        preferred_element_type=F32,
    )
    targets = lax.iota(jnp.int32, CH_BINS // evt_count * evt_count // BLK)
    select = (blocks[None, :] == targets[:, None]).astype(F32)
    block_term = jnp.einsum("qk,ktv->qtv", select, products, precision=HI)
    summed = lax.psum_scatter(
        block_term.reshape(CH_BINS, var_local).astype(BF), "evt", scatter_dimension=0, tiled=True
    )
    return lax.all_to_all(summed, "var", split_axis=0, concat_axis=1, tiled=True).astype(F32)


def fit_any(templates, mixing, expected, excess):
    jacobian = jnp.dot(templates, mixing, precision=HI)
    inverse = 1.0 / expected
    gram = lax.dot_general(
        jacobian * inverse[:, None], jacobian, (((0,), (0,)), ((), ())), precision=HI
    )
    gradient = jnp.dot(excess * inverse, jacobian, precision=HI)
    packed = jnp.zeros((PACKED, NUIS), F32)
    for i in range(SIDE):
        for j in range(i, SIDE):
            row, lane = packed_at(i, j)
            block = gram[i * BLK : (i + 1) * BLK, j * BLK : (j + 1) * BLK]
            packed = packed.at[row : row + BLK, lane : lane + BLK].set(block)
        row, lane = grad_at(i)
        packed = packed.at[row : row + 8, lane : lane + BLK].set(
            gradient[None, i * BLK : (i + 1) * BLK]
        )
    return packed


def shards(
    variation_weights,
    bin_response,
    bin_block,
    variation_coefficient,
    nuisance_index,
    expected,
    excess_counts,
):
    weights = variation_weights[0]
    response = bin_response[0]
    blocks = bin_block[0]
    mixing = (nuisance_index[:, None] == lax.iota(jnp.int32, NUIS)[None, :]).astype(
        F32
    ) * variation_coefficient[:, None]
    if lax.axis_size("evt") == 4 and lax.axis_size("var") == 2:
        own, other = exchange_line(response, weights, blocks)
        hi = mixing.astype(BF)
        lo = (mixing - hi.astype(F32)).astype(BF)
        place = lax.axis_index("var").astype(jnp.int32).reshape(1)
        templates, gram = fit_of(own, other, place, hi, lo, expected[0], excess_counts[0])
        return (templates, pulls_summed(gram))
    else:
        templates = exchange_any(response, weights, blocks)
        gram = fit_any(templates, mixing, expected[0], excess_counts[0])
        templates = templates[None]
    gram = lax.psum(gram, ("evt", "var", "chan"))
    return (templates, pulls_of(gram))


def solution(mesh):
    placed = (
        P("chan", ("grp", "evt"), "var"),
        P("chan", ("grp", "evt"), None),
        P("chan", ("grp", "evt")),
        P(),
        P(),
        P("chan", ("grp", "evt", "var")),
        P("chan", ("grp", "evt", "var")),
    )
    return jax.shard_map(
        shards,
        mesh=mesh,
        in_specs=placed,
        out_specs=(P("chan", ("grp", "evt", "var"), None), P("grp")),
        check_vma=False,
    )
```

```python
import functools

import jax
import jax.numpy as jnp
from jax import lax
from jax.experimental import pallas as pl
from jax.experimental.pallas import tpu as pltpu
from jax.sharding import PartitionSpec as P

BLK = 128
CH_BINS = 16384
NUIS = 512
BF = jnp.bfloat16
F32 = jnp.float32
HI = lax.Precision.HIGHEST


def transposed_dot(a, b):
    return lax.dot_general(a, b, (((0,), (0,)), ((), ())), preferred_element_type=F32)


def product_kernel(group, chunks, response_ref, weights_ref, *out_refs):
    for k in range(group):
        rows = slice(k * BLK, (k + 1) * BLK)
        prod = transposed_dot(response_ref[rows, :], weights_ref[rows, :]).astype(BF)
        for c in range(chunks):
            out_refs[c][k] = prod[:, c * BLK : (c + 1) * BLK]


def products_of(response, weights):
    events, var_local = weights.shape
    nblocks = events // BLK
    chunks = var_local // BLK
    group = 8
    return pl.pallas_call(
        functools.partial(product_kernel, group, chunks),
        grid=(nblocks // group,),
        in_specs=[
            pl.BlockSpec((group * BLK, BLK), lambda i: (i, 0)),
            pl.BlockSpec((group * BLK, var_local), lambda i: (i, 0)),
        ],
        out_specs=[pl.BlockSpec((group, BLK, BLK), lambda i: (i, 0, 0))] * chunks,
        out_shape=[jax.ShapeDtypeStruct((nblocks, BLK, BLK), BF)] * chunks,
        name="products",
    )(response, weights)


def dense_kernel(count, nblocks, with_extra, slots_ref, *refs):
    ins = refs[:count]
    rest = refs[count:]
    if with_extra:
        extra_ref, rest = rest[0], rest[1:]
    *outs, acc = rest
    if with_extra:
        acc[...] = extra_ref[...].astype(F32)
    else:
        acc[...] = jnp.zeros_like(acc)
    for s in range(count):

        def add(k, carry, s=s):
            slot = slots_ref[s * nblocks + k]

            @pl.when(slot >= 0)
            def _():
                acc[slot] = acc[slot] + ins[s][k].astype(F32)

            return carry

        lax.fori_loop(0, nblocks, add, 0)
    at = 0
    for out in outs:
        out[...] = acc[at : at + out.shape[0]].astype(BF)
        at += out.shape[0]


def dense_of(pieces, slots, out_blocks, extra=None):
    nblocks = pieces[0].shape[0]
    total = sum(out_blocks)
    operands = list(pieces) + ([] if extra is None else [extra])
    moved = sum(x.size for x in operands) * 2 + total * BLK * BLK * 2
    return pl.pallas_call(
        functools.partial(dense_kernel, len(pieces), nblocks, extra is not None),
        in_specs=[pl.BlockSpec(memory_space=pltpu.SMEM)]
        + [pl.BlockSpec(memory_space=pltpu.VMEM)] * len(operands),
        out_specs=[pl.BlockSpec(memory_space=pltpu.VMEM)] * len(out_blocks),
        out_shape=[jax.ShapeDtypeStruct((n, BLK, BLK), BF) for n in out_blocks],
        scratch_shapes=[pltpu.VMEM((total, BLK, BLK), F32)],
        compiler_params=pltpu.CompilerParams(vmem_limit_bytes=24 << 20),
        cost_estimate=pl.CostEstimate(flops=moved * 4, bytes_accessed=moved, transcendentals=0),
        name="dense",
    )(slots.reshape(-1), *operands)


def exchange_line(response, weights, blocks):
    z = lax.axis_index("evt")
    x = lax.axis_index("var")
    per_evt = CH_BINS // BLK // 4
    half = per_evt // 2
    pieces = products_of(response, weights)
    nothing = jnp.full_like(blocks, -1)
    ids_right1 = lax.ppermute(blocks, "evt", [(0, 1), (1, 2)])
    ids_left1 = lax.ppermute(blocks, "evt", [(3, 2), (2, 1)])
    ids_right2 = lax.ppermute(ids_right1, "evt", [(1, 2)])
    ids_left2 = lax.ppermute(ids_left1, "evt", [(2, 1)])
    middle = (z == 1) | (z == 2)

    sources = jnp.stack(
        [
            blocks,
            jnp.where(middle, ids_right1, nothing),
            jnp.where(middle, ids_left1, nothing),
            jnp.where(z == 2, ids_right2, nothing),
            jnp.where(z == 1, ids_left2, nothing),
        ]
    )
    rel = sources - z * per_evt
    inside = (sources >= 0) & (rel >= 0) & (rel < per_evt)
    final_slots = jnp.where(inside, (rel + x * half) % per_evt, -1)
    end = jnp.where(z == 1, 0, 3)
    rel_end = sources - end * per_evt
    from_left = jnp.array([1, 1, 0, 1, 0], jnp.int32)[:, None]
    from_right = jnp.array([1, 0, 1, 0, 1], jnp.int32)[:, None]
    use = jnp.where(z == 1, from_right, jnp.where(z == 2, from_left, 0))
    inside_end = (use > 0) & (sources >= 0) & (rel_end >= 0) & (rel_end < per_evt)
    end_slots = jnp.where(inside_end, (rel_end + x * half) % per_evt, -1)

    own, other = [], []
    first_hops, second_hops, to_ends, ends = [], [], [], []
    for c, piece in enumerate(pieces):
        ahead = first_hops[c - 1 : c] + second_hops[: max(c - 1, 0)][-1:]
        if ahead:
            piece, _ = lax.optimization_barrier((piece, ahead))
        right1 = lax.ppermute(piece, "evt", [(0, 1), (1, 2)])
        left1 = lax.ppermute(piece, "evt", [(3, 2), (2, 1)])
        if c >= 2:
            right1, left1, _, _ = lax.optimization_barrier(
                (right1, left1, to_ends[c - 2], ends[: c - 2])
            )
        right2 = lax.ppermute(right1, "evt", [(1, 2)])
        left2 = lax.ppermute(left1, "evt", [(2, 1)])
        first_hops.append((right1, left1))
        second_hops.append((right2, left2))
        buffers = [piece, right1, left1, right2, left2]
        if c >= 2:
            buffers, _ = lax.optimization_barrier((buffers, other[: c - 1]))
        (to_end,) = dense_of(buffers, end_slots, [per_evt])
        to_ends.append(to_end)
        at_end = lax.ppermute(to_end, "evt", [(1, 0), (2, 3)])
        ends.append(at_end)
        mine, theirs = dense_of(buffers, final_slots, [half, half], extra=at_end)
        own.append(mine)
        other.append(lax.ppermute(theirs, "var", [(0, 1), (1, 0)]))
    return own, other


SIDE = NUIS // BLK
PACKED = 384


def packed_at(i, j):
    n = sum(SIDE - k for k in range(i)) + j - i
    return n // SIDE * BLK, n % SIDE * BLK


def grad_at(i):
    n = SIDE * (SIDE + 1) // 2
    return n // SIDE * BLK + 8 * i, n % SIDE * BLK


def column_of(row):
    return jnp.broadcast_to(row, (BLK, row.shape[1])).T


def fit_kernel(chunks, tile, *refs):
    own, other = refs[:chunks], refs[chunks : 2 * chunks]
    place_ref, hi_ref, lo_ref, expected_ref, excess_ref, out_ref, gram_ref = refs[2 * chunks :]
    jac = jnp.zeros((tile, NUIS), F32)
    width = chunks * BLK
    for c in range(2 * chunks):
        if c < chunks:
            piece = own[c][...]
            at = place_ref[0] * width + c * BLK
        else:
            piece = other[c - chunks][...]
            at = (1 - place_ref[0]) * width + (c - chunks) * BLK
        at = pl.multiple_of(at, BLK)
        piece = piece.reshape(tile, BLK)
        out_ref[0, :, pl.ds(at, BLK)] = piece.astype(F32)
    temp = out_ref[0].astype(BF)
    jac = jnp.dot(temp, hi_ref[...], preferred_element_type=F32)
    jac = jac + jnp.dot(temp, lo_ref[...], preferred_element_type=F32)
    inverse = 1.0 / expected_ref[0]
    scale = jnp.concatenate([column_of(inverse)] * (NUIS // BLK), axis=1)
    pull = jnp.concatenate([column_of(inverse * excess_ref[0])] * (NUIS // BLK), axis=1)
    scaled = jac * scale
    jh = jac.astype(BF)
    jl = (jac - jh.astype(F32)).astype(BF)
    sh = scaled.astype(BF)
    sl = (scaled - sh.astype(F32)).astype(BF)
    grad = jnp.sum(jac * pull, axis=0, keepdims=True)

    @pl.when(pl.program_id(0) == 0)
    def _():
        gram_ref[...] = jnp.zeros_like(gram_ref)

    for i in range(SIDE):
        left = slice(i * BLK, (i + 1) * BLK)
        right = slice(i * BLK, NUIS)
        part = transposed_dot(sh[:, left], jh[:, right])
        part = part + transposed_dot(sh[:, left], jl[:, right])
        part = part + transposed_dot(sl[:, left], jh[:, right])
        for j in range(i, SIDE):
            row, lane = packed_at(i, j)
            gram_ref[row : row + BLK, lane : lane + BLK] += part[:, (j - i) * BLK : (j - i + 1) * BLK]
        row, lane = grad_at(i)
        gram_ref[row : row + 8, lane : lane + BLK] += jnp.broadcast_to(grad[:, left], (8, BLK))


def fit_of(own, other, place, hi, lo, expected, excess):
    chunks = len(own)
    bins = own[0].shape[0] * BLK
    tile = 512
    variations = 2 * chunks * BLK
    blocks = tile // BLK
    chunk_spec = pl.BlockSpec((blocks, BLK, BLK), lambda i: (i, 0, 0))
    row_spec = pl.BlockSpec((1, 1, tile), lambda i: (i, 0, 0))
    mix_spec = pl.BlockSpec((variations, NUIS), lambda i: (0, 0))
    return pl.pallas_call(
        functools.partial(fit_kernel, chunks, tile),
        grid=(bins // tile,),
        in_specs=[chunk_spec] * (2 * chunks)
        + [pl.BlockSpec(memory_space=pltpu.SMEM), mix_spec, mix_spec, row_spec, row_spec],
        out_specs=[
            pl.BlockSpec((1, tile, variations), lambda i: (0, i, 0)),
            pl.BlockSpec((PACKED, NUIS), lambda i: (0, 0)),
        ],
        out_shape=[
            jax.ShapeDtypeStruct((1, bins, variations), F32),
            jax.ShapeDtypeStruct((PACKED, NUIS), F32),
        ],
        compiler_params=pltpu.CompilerParams(vmem_limit_bytes=40 << 20),
        name="fit",
    )(
        *own,
        *other,
        place,
        hi,
        lo,
        expected.reshape(bins // tile, 1, tile),
        excess.reshape(bins // tile, 1, tile),
    )


def swept(a):
    rows = lax.broadcasted_iota(jnp.int32, (BLK, BLK), 0)
    lanes = lax.broadcasted_iota(jnp.int32, (BLK, BLK), 1)
    for k in range(BLK):
        row = a[k : k + 1, :]
        col = a[:, k : k + 1]
        inv = 1.0 / a[k : k + 1, k : k + 1]
        lane_k = lanes[:1] == k
        scaled_row = jnp.where(lane_k, -inv, row * inv)
        kept = jnp.where(lane_k, 0.0, a)
        a = jnp.where(rows == k, scaled_row, kept - col * jnp.where(lane_k, -inv, row * inv))
    return -a


def solve_packed(packed_ref, out_ref, mat_ref):
    rows = lax.broadcasted_iota(jnp.int32, (BLK, BLK), 0)
    lanes = lax.broadcasted_iota(jnp.int32, (BLK, BLK), 1)
    on_diagonal = rows == lanes
    diagonal = []
    for i in range(SIDE):
        at = slice(i * BLK, (i + 1) * BLK)
        for j in range(i, SIDE):
            row, lane = packed_at(i, j)
            block = packed_ref[row : row + BLK, lane : lane + BLK]
            if i == j:
                block = block + jnp.where(on_diagonal, 1.0, 0.0)
                diagonal.append(
                    jnp.sum(jnp.where(on_diagonal, block, 0.0), axis=0, keepdims=True)
                )
                mat_ref[at, at] = block
            else:
                to = slice(j * BLK, (j + 1) * BLK)
                mat_ref[at, to] = block
                mat_ref[to, at] = block.T
        row, lane = grad_at(i)
        mat_ref[at, NUIS:] = column_of(packed_ref[row : row + 1, lane : lane + BLK])
    diagonal = jnp.concatenate(diagonal, axis=1)

    def eliminate(j, carry):
        at = pl.multiple_of(j * BLK, BLK)
        inverse = swept(mat_ref[pl.ds(at, BLK), pl.ds(at, BLK)])
        pivot = jnp.dot(
            inverse, mat_ref[pl.ds(at, BLK), :], precision=HI, preferred_element_type=F32
        )
        factor = mat_ref[:, pl.ds(at, BLK)]
        block_of_row = lax.broadcasted_iota(jnp.int32, (NUIS, BLK), 0) // BLK
        factor = jnp.where(block_of_row == j, 0.0, factor)
        mat_ref[...] = mat_ref[...] - jnp.dot(
            factor, pivot, precision=HI, preferred_element_type=F32
        )
        mat_ref[pl.ds(at, BLK), :] = pivot
        return carry

    lax.fori_loop(0, NUIS // BLK, eliminate, 0)
    steps = mat_ref[:, NUIS:].T[:8]
    out_ref[...] = steps * jnp.sqrt(diagonal)


def summed_solve_kernel(
    gram_ref, out_ref, buf, from_chan, from_var, from_evt, res, mat_ref, send_sem, recv_sem
):
    c, x, z = lax.axis_index("chan"), lax.axis_index("var"), lax.axis_index("evt")
    half, quarter, part = PACKED // 2, PACKED // 4, PACKED // 16
    over_chan, over_var = {"chan": 1 - c}, {"var": 1 - x}
    over_evt = [{"evt": lax.rem(z + d, 4)} for d in (1, 2, 3)]
    mesh_ids = pl.DeviceIdType.MESH

    barrier = pltpu.get_barrier_semaphore()
    for other in [over_chan, over_var] + over_evt:
        pl.semaphore_signal(barrier, inc=1, device_id=other, device_id_type=mesh_ids)
    pl.semaphore_wait(barrier, 5)

    def copy(n, src, dst, other):
        return pltpu.make_async_remote_copy(
            src_ref=src,
            dst_ref=dst,
            send_sem=send_sem.at[n],
            recv_sem=recv_sem.at[n],
            device_id=other,
            device_id_type=mesh_ids,
        )

    def rows(start, count):
        return pl.ds(pl.multiple_of(start, 8), count)

    half_at = c * half
    step = copy(0, gram_ref.at[rows((1 - c) * half, half)], from_chan, over_chan)
    step.start()
    step.wait()
    buf[...] = gram_ref[rows(half_at, half), :] + from_chan[...]
    step = copy(1, buf.at[rows((1 - x) * quarter, quarter)], from_var, over_var)
    step.start()
    step.wait()
    mine = buf.at[rows(x * quarter, quarter)]
    mine[...] = mine[...] + from_var[...]
    steps = []
    for d, other in enumerate(over_evt):
        target = lax.rem(z + d + 1, 4)
        at = rows(x * quarter + target * part, part)
        steps.append(copy(2 + d, buf.at[at], from_evt.at[d], other))
    for step in steps:
        step.start()
    for step in steps:
        step.wait()
    own_at = rows(half_at + x * quarter + z * part, part)
    total = buf[rows(x * quarter + z * part, part), :] + from_evt[0]
    res[own_at, :] = total + from_evt[1] + from_evt[2]
    steps = [copy(5 + d, res.at[own_at], res.at[own_at], o) for d, o in enumerate(over_evt)]
    for step in steps:
        step.start()
    for step in steps:
        step.wait()
    quarter_at = rows(half_at + x * quarter, quarter)
    step = copy(8, res.at[quarter_at], res.at[quarter_at], over_var)
    step.start()
    step.wait()
    half_rows = rows(half_at, half)
    step = copy(9, res.at[half_rows], res.at[half_rows], over_chan)
    step.start()
    step.wait()
    solve_packed(res, out_ref, mat_ref)


def pulls_summed(gram):
    half, quarter, part = PACKED // 2, PACKED // 4, PACKED // 16
    return pl.pallas_call(
        summed_solve_kernel,
        in_specs=[pl.BlockSpec(memory_space=pltpu.VMEM)],
        out_specs=pl.BlockSpec(memory_space=pltpu.VMEM),
        out_shape=jax.ShapeDtypeStruct((8, NUIS), F32),
        scratch_shapes=[
            pltpu.VMEM((half, NUIS), F32),
            pltpu.VMEM((half, NUIS), F32),
            pltpu.VMEM((quarter, NUIS), F32),
            pltpu.VMEM((3, part, NUIS), F32),
            pltpu.VMEM((PACKED, NUIS), F32),
            pltpu.VMEM((NUIS, NUIS + BLK), F32),
            pltpu.SemaphoreType.DMA((10,)),
            pltpu.SemaphoreType.DMA((10,)),
        ],
        compiler_params=pltpu.CompilerParams(
            collective_id=0, has_side_effects=True, vmem_limit_bytes=24 << 20
        ),
        name="sum_solve",
    )(gram)[0]


def pulls_of(gram):
    out = pl.pallas_call(
        solve_packed,
        in_specs=[pl.BlockSpec(memory_space=pltpu.VMEM)],
        out_specs=pl.BlockSpec(memory_space=pltpu.VMEM),
        out_shape=jax.ShapeDtypeStruct((8, NUIS), F32),
        scratch_shapes=[pltpu.VMEM((NUIS, NUIS + BLK), F32)],
        compiler_params=pltpu.CompilerParams(vmem_limit_bytes=24 << 20),
        name="solve",
    )(gram)
    return out[0]


def exchange_any(response, weights, blocks):
    evt_count = lax.axis_size("evt")
    nblocks = blocks.shape[0]
    var_local = weights.shape[1]
    products = jnp.einsum(
        "ket,kev->ktv",
        response.reshape(nblocks, BLK, BLK),
        weights.reshape(nblocks, BLK, var_local),
        preferred_element_type=F32,
    )
    targets = lax.iota(jnp.int32, CH_BINS // evt_count * evt_count // BLK)
    select = (blocks[None, :] == targets[:, None]).astype(F32)
    block_term = jnp.einsum("qk,ktv->qtv", select, products, precision=HI)
    summed = lax.psum_scatter(
        block_term.reshape(CH_BINS, var_local).astype(BF), "evt", scatter_dimension=0, tiled=True
    )
    return lax.all_to_all(summed, "var", split_axis=0, concat_axis=1, tiled=True).astype(F32)


def fit_any(templates, mixing, expected, excess):
    jacobian = jnp.dot(templates, mixing, precision=HI)
    inverse = 1.0 / expected
    gram = lax.dot_general(
        jacobian * inverse[:, None], jacobian, (((0,), (0,)), ((), ())), precision=HI
    )
    gradient = jnp.dot(excess * inverse, jacobian, precision=HI)
    packed = jnp.zeros((PACKED, NUIS), F32)
    for i in range(SIDE):
        for j in range(i, SIDE):
            row, lane = packed_at(i, j)
            block = gram[i * BLK : (i + 1) * BLK, j * BLK : (j + 1) * BLK]
            packed = packed.at[row : row + BLK, lane : lane + BLK].set(block)
        row, lane = grad_at(i)
        packed = packed.at[row : row + 8, lane : lane + BLK].set(
            gradient[None, i * BLK : (i + 1) * BLK]
        )
    return packed


def shards(
    variation_weights,
    bin_response,
    bin_block,
    variation_coefficient,
    nuisance_index,
    expected,
    excess_counts,
):
    weights = variation_weights[0]
    response = bin_response[0]
    blocks = bin_block[0]
    mixing = (nuisance_index[:, None] == lax.iota(jnp.int32, NUIS)[None, :]).astype(
        F32
    ) * variation_coefficient[:, None]
    if lax.axis_size("evt") == 4 and lax.axis_size("var") == 2:
        own, other = exchange_line(response, weights, blocks)
        hi = mixing.astype(BF)
        lo = (mixing - hi.astype(F32)).astype(BF)
        place = lax.axis_index("var").astype(jnp.int32).reshape(1)
        templates, gram = fit_of(own, other, place, hi, lo, expected[0], excess_counts[0])
        return (templates, pulls_summed(gram))
    else:
        templates = exchange_any(response, weights, blocks)
        gram = fit_any(templates, mixing, expected[0], excess_counts[0])
        templates = templates[None]
    gram = lax.psum(gram, ("evt", "var", "chan"))
    return (templates, pulls_of(gram))


def solution(mesh):
    placed = (
        P("chan", ("grp", "evt"), "var"),
        P("chan", ("grp", "evt"), None),
        P("chan", ("grp", "evt")),
        P(),
        P(),
        P("chan", ("grp", "evt", "var")),
        P("chan", ("grp", "evt", "var")),
    )
    return jax.shard_map(
        shards,
        mesh=mesh,
        in_specs=placed,
        out_specs=(P("chan", ("grp", "evt", "var"), None), P("grp")),
        check_vma=False,
    )
```

```python
import functools

import jax
import jax.numpy as jnp
from jax import lax
from jax.experimental import pallas as pl
from jax.experimental.pallas import tpu as pltpu
from jax.sharding import PartitionSpec as P

BLK = 128
CH_BINS = 16384
NUIS = 512
BF = jnp.bfloat16
F32 = jnp.float32
HI = lax.Precision.HIGHEST


def transposed_dot(a, b):
    return lax.dot_general(a, b, (((0,), (0,)), ((), ())), preferred_element_type=F32)


def product_kernel(group, chunks, response_ref, weights_ref, *out_refs):
    for k in range(group):
        rows = slice(k * BLK, (k + 1) * BLK)
        prod = transposed_dot(response_ref[rows, :], weights_ref[rows, :]).astype(BF)
        for c in range(chunks):
            out_refs[c][k] = prod[:, c * BLK : (c + 1) * BLK]


def products_of(response, weights):
    events, var_local = weights.shape
    nblocks = events // BLK
    chunks = var_local // BLK
    group = 8
    return pl.pallas_call(
        functools.partial(product_kernel, group, chunks),
        grid=(nblocks // group,),
        in_specs=[
            pl.BlockSpec((group * BLK, BLK), lambda i: (i, 0)),
            pl.BlockSpec((group * BLK, var_local), lambda i: (i, 0)),
        ],
        out_specs=[pl.BlockSpec((group, BLK, BLK), lambda i: (i, 0, 0))] * chunks,
        out_shape=[jax.ShapeDtypeStruct((nblocks, BLK, BLK), BF)] * chunks,
        name="products",
    )(response, weights)


def dense_kernel(count, nblocks, with_extra, slots_ref, *refs):
    ins = refs[:count]
    rest = refs[count:]
    if with_extra:
        extra_ref, rest = rest[0], rest[1:]
    *outs, acc = rest
    if with_extra:
        acc[...] = extra_ref[...].astype(F32)
    else:
        acc[...] = jnp.zeros_like(acc)
    for s in range(count):

        def add(k, carry, s=s):
            slot = slots_ref[s * nblocks + k]

            @pl.when(slot >= 0)
            def _():
                acc[slot] = acc[slot] + ins[s][k].astype(F32)

            return carry

        lax.fori_loop(0, nblocks, add, 0)
    at = 0
    for out in outs:
        out[...] = acc[at : at + out.shape[0]].astype(BF)
        at += out.shape[0]


def dense_of(pieces, slots, out_blocks, extra=None):
    nblocks = pieces[0].shape[0]
    total = sum(out_blocks)
    operands = list(pieces) + ([] if extra is None else [extra])
    moved = sum(x.size for x in operands) * 2 + total * BLK * BLK * 2
    return pl.pallas_call(
        functools.partial(dense_kernel, len(pieces), nblocks, extra is not None),
        in_specs=[pl.BlockSpec(memory_space=pltpu.SMEM)]
        + [pl.BlockSpec(memory_space=pltpu.VMEM)] * len(operands),
        out_specs=[pl.BlockSpec(memory_space=pltpu.VMEM)] * len(out_blocks),
        out_shape=[jax.ShapeDtypeStruct((n, BLK, BLK), BF) for n in out_blocks],
        scratch_shapes=[pltpu.VMEM((total, BLK, BLK), F32)],
        compiler_params=pltpu.CompilerParams(vmem_limit_bytes=24 << 20),
        cost_estimate=pl.CostEstimate(flops=moved * 4, bytes_accessed=moved, transcendentals=0),
        name="dense",
    )(slots.reshape(-1), *operands)


def exchange_line(response, weights, blocks):
    z = lax.axis_index("evt")
    x = lax.axis_index("var")
    per_evt = CH_BINS // BLK // 4
    half = per_evt // 2
    pieces = products_of(response, weights)
    nothing = jnp.full_like(blocks, -1)
    ids_right1 = lax.ppermute(blocks, "evt", [(0, 1), (1, 2)])
    ids_left1 = lax.ppermute(blocks, "evt", [(3, 2), (2, 1)])
    ids_right2 = lax.ppermute(ids_right1, "evt", [(1, 2)])
    ids_left2 = lax.ppermute(ids_left1, "evt", [(2, 1)])
    middle = (z == 1) | (z == 2)

    sources = jnp.stack(
        [
            blocks,
            jnp.where(middle, ids_right1, nothing),
            jnp.where(middle, ids_left1, nothing),
            jnp.where(z == 2, ids_right2, nothing),
            jnp.where(z == 1, ids_left2, nothing),
        ]
    )
    rel = sources - z * per_evt
    inside = (sources >= 0) & (rel >= 0) & (rel < per_evt)
    final_slots = jnp.where(inside, (rel + x * half) % per_evt, -1)
    end = jnp.where(z == 1, 0, 3)
    rel_end = sources - end * per_evt
    from_left = jnp.array([1, 1, 0, 1, 0], jnp.int32)[:, None]
    from_right = jnp.array([1, 0, 1, 0, 1], jnp.int32)[:, None]
    use = jnp.where(z == 1, from_right, jnp.where(z == 2, from_left, 0))
    inside_end = (use > 0) & (sources >= 0) & (rel_end >= 0) & (rel_end < per_evt)
    end_slots = jnp.where(inside_end, (rel_end + x * half) % per_evt, -1)

    own, other = [], []
    first_hops, second_hops, to_ends, ends = [], [], [], []
    for c, piece in enumerate(pieces):
        ahead = first_hops[c - 1 : c] + second_hops[: max(c - 1, 0)][-1:]
        if ahead:
            piece, _ = lax.optimization_barrier((piece, ahead))
        right1 = lax.ppermute(piece, "evt", [(0, 1), (1, 2)])
        left1 = lax.ppermute(piece, "evt", [(3, 2), (2, 1)])
        if c == 0:
            right1, left1, _ = lax.optimization_barrier(
                (right1, left1, (ids_right1, ids_left1))
            )
        if c >= 2:
            right1, left1, _, _ = lax.optimization_barrier(
                (right1, left1, to_ends[c - 2], ends[: c - 2])
            )
        right2 = lax.ppermute(right1, "evt", [(1, 2)])
        left2 = lax.ppermute(left1, "evt", [(2, 1)])
        first_hops.append((right1, left1))
        second_hops.append((right2, left2))
        buffers = [piece, right1, left1, right2, left2]
        if c >= 2:
            buffers, _ = lax.optimization_barrier((buffers, other[: c - 1]))
        (to_end,) = dense_of(buffers, end_slots, [per_evt])
        to_ends.append(to_end)
        at_end = lax.ppermute(to_end, "evt", [(1, 0), (2, 3)])
        ends.append(at_end)
        mine, theirs = dense_of(buffers, final_slots, [half, half], extra=at_end)
        own.append(mine)
        other.append(lax.ppermute(theirs, "var", [(0, 1), (1, 0)]))
    return own, other


SIDE = NUIS // BLK
PACKED = 384


def packed_at(i, j):
    n = sum(SIDE - k for k in range(i)) + j - i
    return n // SIDE * BLK, n % SIDE * BLK


def grad_at(i):
    n = SIDE * (SIDE + 1) // 2
    return n // SIDE * BLK + 8 * i, n % SIDE * BLK


def column_of(row):
    return jnp.broadcast_to(row, (BLK, row.shape[1])).T


def fit_kernel(chunks, tile, *refs):
    own, other = refs[:chunks], refs[chunks : 2 * chunks]
    place_ref, hi_ref, lo_ref, expected_ref, excess_ref, out_ref, gram_ref = refs[2 * chunks :]
    jac = jnp.zeros((tile, NUIS), F32)
    width = chunks * BLK
    for c in range(2 * chunks):
        if c < chunks:
            piece = own[c][...]
            at = place_ref[0] * width + c * BLK
        else:
            piece = other[c - chunks][...]
            at = (1 - place_ref[0]) * width + (c - chunks) * BLK
        at = pl.multiple_of(at, BLK)
        piece = piece.reshape(tile, BLK)
        out_ref[0, :, pl.ds(at, BLK)] = piece.astype(F32)
    temp = out_ref[0].astype(BF)
    jac = jnp.dot(temp, hi_ref[...], preferred_element_type=F32)
    jac = jac + jnp.dot(temp, lo_ref[...], preferred_element_type=F32)
    inverse = 1.0 / expected_ref[0]
    scale = jnp.concatenate([column_of(inverse)] * (NUIS // BLK), axis=1)
    pull = jnp.concatenate([column_of(inverse * excess_ref[0])] * (NUIS // BLK), axis=1)
    scaled = jac * scale
    jh = jac.astype(BF)
    jl = (jac - jh.astype(F32)).astype(BF)
    sh = scaled.astype(BF)
    sl = (scaled - sh.astype(F32)).astype(BF)
    grad = jnp.sum(jac * pull, axis=0, keepdims=True)

    @pl.when(pl.program_id(0) == 0)
    def _():
        gram_ref[...] = jnp.zeros_like(gram_ref)

    for i in range(SIDE):
        left = slice(i * BLK, (i + 1) * BLK)
        right = slice(i * BLK, NUIS)
        part = transposed_dot(sh[:, left], jh[:, right])
        part = part + transposed_dot(sh[:, left], jl[:, right])
        part = part + transposed_dot(sl[:, left], jh[:, right])
        for j in range(i, SIDE):
            row, lane = packed_at(i, j)
            gram_ref[row : row + BLK, lane : lane + BLK] += part[:, (j - i) * BLK : (j - i + 1) * BLK]
        row, lane = grad_at(i)
        gram_ref[row : row + 8, lane : lane + BLK] += jnp.broadcast_to(grad[:, left], (8, BLK))


def fit_of(own, other, place, hi, lo, expected, excess):
    chunks = len(own)
    bins = own[0].shape[0] * BLK
    tile = 512
    variations = 2 * chunks * BLK
    blocks = tile // BLK
    chunk_spec = pl.BlockSpec((blocks, BLK, BLK), lambda i: (i, 0, 0))
    row_spec = pl.BlockSpec((1, 1, tile), lambda i: (i, 0, 0))
    mix_spec = pl.BlockSpec((variations, NUIS), lambda i: (0, 0))
    return pl.pallas_call(
        functools.partial(fit_kernel, chunks, tile),
        grid=(bins // tile,),
        in_specs=[chunk_spec] * (2 * chunks)
        + [pl.BlockSpec(memory_space=pltpu.SMEM), mix_spec, mix_spec, row_spec, row_spec],
        out_specs=[
            pl.BlockSpec((1, tile, variations), lambda i: (0, i, 0)),
            pl.BlockSpec((PACKED, NUIS), lambda i: (0, 0)),
        ],
        out_shape=[
            jax.ShapeDtypeStruct((1, bins, variations), F32),
            jax.ShapeDtypeStruct((PACKED, NUIS), F32),
        ],
        compiler_params=pltpu.CompilerParams(vmem_limit_bytes=40 << 20),
        name="fit",
    )(
        *own,
        *other,
        place,
        hi,
        lo,
        expected.reshape(bins // tile, 1, tile),
        excess.reshape(bins // tile, 1, tile),
    )


def swept(a):
    rows = lax.broadcasted_iota(jnp.int32, (BLK, BLK), 0)
    lanes = lax.broadcasted_iota(jnp.int32, (BLK, BLK), 1)
    for k in range(BLK):
        row = a[k : k + 1, :]
        col = a[:, k : k + 1]
        inv = 1.0 / a[k : k + 1, k : k + 1]
        lane_k = lanes[:1] == k
        scaled_row = jnp.where(lane_k, -inv, row * inv)
        kept = jnp.where(lane_k, 0.0, a)
        a = jnp.where(rows == k, scaled_row, kept - col * jnp.where(lane_k, -inv, row * inv))
    return -a


def solve_packed(packed_ref, out_ref, mat_ref):
    rows = lax.broadcasted_iota(jnp.int32, (BLK, BLK), 0)
    lanes = lax.broadcasted_iota(jnp.int32, (BLK, BLK), 1)
    on_diagonal = rows == lanes
    diagonal = []
    for i in range(SIDE):
        at = slice(i * BLK, (i + 1) * BLK)
        for j in range(i, SIDE):
            row, lane = packed_at(i, j)
            block = packed_ref[row : row + BLK, lane : lane + BLK]
            if i == j:
                block = block + jnp.where(on_diagonal, 1.0, 0.0)
                diagonal.append(
                    jnp.sum(jnp.where(on_diagonal, block, 0.0), axis=0, keepdims=True)
                )
                mat_ref[at, at] = block
            else:
                to = slice(j * BLK, (j + 1) * BLK)
                mat_ref[at, to] = block
                mat_ref[to, at] = block.T
        row, lane = grad_at(i)
        mat_ref[at, NUIS:] = column_of(packed_ref[row : row + 1, lane : lane + BLK])
    diagonal = jnp.concatenate(diagonal, axis=1)

    def eliminate(j, carry):
        at = pl.multiple_of(j * BLK, BLK)
        inverse = swept(mat_ref[pl.ds(at, BLK), pl.ds(at, BLK)])
        pivot = jnp.dot(
            inverse, mat_ref[pl.ds(at, BLK), :], precision=HI, preferred_element_type=F32
        )
        factor = mat_ref[:, pl.ds(at, BLK)]
        block_of_row = lax.broadcasted_iota(jnp.int32, (NUIS, BLK), 0) // BLK
        factor = jnp.where(block_of_row == j, 0.0, factor)
        mat_ref[...] = mat_ref[...] - jnp.dot(
            factor, pivot, precision=HI, preferred_element_type=F32
        )
        mat_ref[pl.ds(at, BLK), :] = pivot
        return carry

    lax.fori_loop(0, NUIS // BLK, eliminate, 0)
    steps = mat_ref[:, NUIS:].T[:8]
    out_ref[...] = steps * jnp.sqrt(diagonal)


def summed_solve_kernel(
    gram_ref, out_ref, buf, from_chan, from_var, from_evt, res, mat_ref, send_sem, recv_sem
):
    c, x, z = lax.axis_index("chan"), lax.axis_index("var"), lax.axis_index("evt")
    half, quarter, part = PACKED // 2, PACKED // 4, PACKED // 16
    over_chan, over_var = {"chan": 1 - c}, {"var": 1 - x}
    over_evt = [{"evt": lax.rem(z + d, 4)} for d in (1, 2, 3)]
    mesh_ids = pl.DeviceIdType.MESH

    barrier = pltpu.get_barrier_semaphore()
    for other in [over_chan, over_var] + over_evt:
        pl.semaphore_signal(barrier, inc=1, device_id=other, device_id_type=mesh_ids)
    pl.semaphore_wait(barrier, 5)

    def copy(n, src, dst, other):
        return pltpu.make_async_remote_copy(
            src_ref=src,
            dst_ref=dst,
            send_sem=send_sem.at[n],
            recv_sem=recv_sem.at[n],
            device_id=other,
            device_id_type=mesh_ids,
        )

    def rows(start, count):
        return pl.ds(pl.multiple_of(start, 8), count)

    half_at = c * half
    step = copy(0, gram_ref.at[rows((1 - c) * half, half)], from_chan, over_chan)
    step.start()
    step.wait()
    buf[...] = gram_ref[rows(half_at, half), :] + from_chan[...]
    step = copy(1, buf.at[rows((1 - x) * quarter, quarter)], from_var, over_var)
    step.start()
    step.wait()
    mine = buf.at[rows(x * quarter, quarter)]
    mine[...] = mine[...] + from_var[...]
    steps = []
    for d, other in enumerate(over_evt):
        target = lax.rem(z + d + 1, 4)
        at = rows(x * quarter + target * part, part)
        steps.append(copy(2 + d, buf.at[at], from_evt.at[d], other))
    for step in steps:
        step.start()
    for step in steps:
        step.wait()
    own_at = rows(half_at + x * quarter + z * part, part)
    total = buf[rows(x * quarter + z * part, part), :] + from_evt[0]
    res[own_at, :] = total + from_evt[1] + from_evt[2]
    steps = [copy(5 + d, res.at[own_at], res.at[own_at], o) for d, o in enumerate(over_evt)]
    for step in steps:
        step.start()
    for step in steps:
        step.wait()
    quarter_at = rows(half_at + x * quarter, quarter)
    step = copy(8, res.at[quarter_at], res.at[quarter_at], over_var)
    step.start()
    step.wait()
    half_rows = rows(half_at, half)
    step = copy(9, res.at[half_rows], res.at[half_rows], over_chan)
    step.start()
    step.wait()
    solve_packed(res, out_ref, mat_ref)


def pulls_summed(gram):
    half, quarter, part = PACKED // 2, PACKED // 4, PACKED // 16
    return pl.pallas_call(
        summed_solve_kernel,
        in_specs=[pl.BlockSpec(memory_space=pltpu.VMEM)],
        out_specs=pl.BlockSpec(memory_space=pltpu.VMEM),
        out_shape=jax.ShapeDtypeStruct((8, NUIS), F32),
        scratch_shapes=[
            pltpu.VMEM((half, NUIS), F32),
            pltpu.VMEM((half, NUIS), F32),
            pltpu.VMEM((quarter, NUIS), F32),
            pltpu.VMEM((3, part, NUIS), F32),
            pltpu.VMEM((PACKED, NUIS), F32),
            pltpu.VMEM((NUIS, NUIS + BLK), F32),
            pltpu.SemaphoreType.DMA((10,)),
            pltpu.SemaphoreType.DMA((10,)),
        ],
        compiler_params=pltpu.CompilerParams(
            collective_id=0, has_side_effects=True, vmem_limit_bytes=24 << 20
        ),
        name="sum_solve",
    )(gram)[0]


def pulls_of(gram):
    out = pl.pallas_call(
        solve_packed,
        in_specs=[pl.BlockSpec(memory_space=pltpu.VMEM)],
        out_specs=pl.BlockSpec(memory_space=pltpu.VMEM),
        out_shape=jax.ShapeDtypeStruct((8, NUIS), F32),
        scratch_shapes=[pltpu.VMEM((NUIS, NUIS + BLK), F32)],
        compiler_params=pltpu.CompilerParams(vmem_limit_bytes=24 << 20),
        name="solve",
    )(gram)
    return out[0]


def exchange_any(response, weights, blocks):
    evt_count = lax.axis_size("evt")
    nblocks = blocks.shape[0]
    var_local = weights.shape[1]
    products = jnp.einsum(
        "ket,kev->ktv",
        response.reshape(nblocks, BLK, BLK),
        weights.reshape(nblocks, BLK, var_local),
        preferred_element_type=F32,
    )
    targets = lax.iota(jnp.int32, CH_BINS // evt_count * evt_count // BLK)
    select = (blocks[None, :] == targets[:, None]).astype(F32)
    block_term = jnp.einsum("qk,ktv->qtv", select, products, precision=HI)
    summed = lax.psum_scatter(
        block_term.reshape(CH_BINS, var_local).astype(BF), "evt", scatter_dimension=0, tiled=True
    )
    return lax.all_to_all(summed, "var", split_axis=0, concat_axis=1, tiled=True).astype(F32)


def fit_any(templates, mixing, expected, excess):
    jacobian = jnp.dot(templates, mixing, precision=HI)
    inverse = 1.0 / expected
    gram = lax.dot_general(
        jacobian * inverse[:, None], jacobian, (((0,), (0,)), ((), ())), precision=HI
    )
    gradient = jnp.dot(excess * inverse, jacobian, precision=HI)
    packed = jnp.zeros((PACKED, NUIS), F32)
    for i in range(SIDE):
        for j in range(i, SIDE):
            row, lane = packed_at(i, j)
            block = gram[i * BLK : (i + 1) * BLK, j * BLK : (j + 1) * BLK]
            packed = packed.at[row : row + BLK, lane : lane + BLK].set(block)
        row, lane = grad_at(i)
        packed = packed.at[row : row + 8, lane : lane + BLK].set(
            gradient[None, i * BLK : (i + 1) * BLK]
        )
    return packed


def shards(
    variation_weights,
    bin_response,
    bin_block,
    variation_coefficient,
    nuisance_index,
    expected,
    excess_counts,
):
    weights = variation_weights[0]
    response = bin_response[0]
    blocks = bin_block[0]
    mixing = (nuisance_index[:, None] == lax.iota(jnp.int32, NUIS)[None, :]).astype(
        F32
    ) * variation_coefficient[:, None]
    if lax.axis_size("evt") == 4 and lax.axis_size("var") == 2:
        own, other = exchange_line(response, weights, blocks)
        hi = mixing.astype(BF)
        lo = (mixing - hi.astype(F32)).astype(BF)
        place = lax.axis_index("var").astype(jnp.int32).reshape(1)
        templates, gram = fit_of(own, other, place, hi, lo, expected[0], excess_counts[0])
        return (templates, pulls_summed(gram))
    else:
        templates = exchange_any(response, weights, blocks)
        gram = fit_any(templates, mixing, expected[0], excess_counts[0])
        templates = templates[None]
    gram = lax.psum(gram, ("evt", "var", "chan"))
    return (templates, pulls_of(gram))


def solution(mesh):
    placed = (
        P("chan", ("grp", "evt"), "var"),
        P("chan", ("grp", "evt"), None),
        P("chan", ("grp", "evt")),
        P(),
        P(),
        P("chan", ("grp", "evt", "var")),
        P("chan", ("grp", "evt", "var")),
    )
    return jax.shard_map(
        shards,
        mesh=mesh,
        in_specs=placed,
        out_specs=(P("chan", ("grp", "evt", "var"), None), P("grp")),
        check_vma=False,
    )
```
